512 devices in a mesh: dp: 128 (over z, y, core), shard: 4 (over x).
Axes of the slice: x: 4, y: 4, z: 16, core: 2. Of those that a mesh axis runs over, the one named last changes fastest.
Arguments:
- key_grad: bfloat16 [128, 512, 2560], P('dp', 'shard'), may hold values from -90 to 90
- key_error: float32 [128, 512, 2560], P('dp', 'shard'), may hold values from -4 to 4
- router_grad: bfloat16 [128, 64, 2560], P('dp', 'shard'), may hold values from -90 to 90
- router_error: float32 [128, 64, 2560], P('dp', 'shard'), may hold values from -4 to 4
- norm_grad: bfloat16 [128, 2, 2560], P('dp', None, 'shard'), may hold values from -8 to 8
- key_basis: float32 [32, 2560], replicated, may hold values from -6 to 6
- router_basis: float32 [32, 2560], replicated, may hold values from -6 to 6
- key_momentum: float32 [512, 2560], P('shard', 'dp'), may hold values from -4 to 4
- key_weight: float32 [512, 2560], P('shard', 'dp'), may hold values from -4 to 4
- router_momentum: float32 [64, 2560], P('shard', 'dp'), may hold values from -4 to 4
- router_weight: float32 [64, 2560], P('shard', 'dp'), may hold values from -4 to 4
- norm_momentum: float32 [2, 2560], P(None, 'shard'), may hold values from -4 to 4
- norm_weight: float32 [2, 2560], P(None, 'shard'), may hold values from 0.5 to 1.5
Outputs:
- key_carry: float32 [128, 512, 2560], P('dp', 'shard')
- router_carry: float32 [128, 64, 2560], P('dp', 'shard')
- key_velocity: float32 [512, 2560], P('shard', 'dp')
- key_master: float32 [512, 2560], P('shard', 'dp')
- key_params: bfloat16 [512, 2560], P(None, 'dp')
- router_velocity: float32 [64, 2560], P('shard', 'dp')
- router_master: float32 [64, 2560], P('shard', 'dp')
- router_params: bfloat16 [64, 2560], P(None, 'dp')
- norm_velocity: float32 [2, 2560], P(None, 'shard')
- norm_master: float32 [2, 2560], P(None, 'shard')
- norm_params: bfloat16 [2, 2560], replicated
The draws below stay inside these ranges and needn't reach their ends.
All inputs are finite; a program needn't handle non-finite values.
Results may differ from the reference program's by a relative error of at most 0.008.
Values may be sent and summed in bfloat16 or wider, within the bound.
No kernel may reach another device: no remote copies, remote signals or barrier semaphores. Data moves between devices by JAX's collectives and lax.ppermute only.
A program may use at most 64 MiB of HBM per device.

```python
import jax
import jax.numpy as jnp
from jax import lax

WIDTH = 2560
KEY_ROWS = 512
EXPERTS = 64
NORM_VECS = 2
FACTOR_RANK = 32
ROOT_STEPS = 4
REPLICAS = 128
N_DP = 128


def gradient_draw(key, replicas, row_count, col_count):
    noise_key, common_key, row_key, col_key, replica_key = jax.random.split(key, 5)
    noise_part = jnp.clip(jax.random.normal(noise_key, (replicas, row_count, col_count), jnp.float32), -5.0, 5.0)
    common = jnp.clip(jax.random.normal(common_key, (1, row_count, col_count), jnp.float32), -5.0, 5.0)
    replica_scale = 10.0 ** jax.random.uniform(replica_key, (replicas, 1, 1), jnp.float32, 0.0, 1.0)
    mixed = 0.2 * common + replica_scale * noise_part
    jitter = jax.random.uniform(row_key, (row_count,), jnp.float32, -0.15, 0.15)
    row_scale = 10.0 ** (jnp.arange(row_count, dtype=jnp.float32) / row_count + jitter)
    col_scale = 10.0 ** jax.random.uniform(col_key, (col_count,), jnp.float32, 0.0, 1.0)
    return 0.012 * mixed * row_scale[None, :, None] * col_scale[None, None, :]


def draw_key_grad(key, part):
    return gradient_draw(key, REPLICAS, KEY_ROWS, WIDTH).astype(jnp.bfloat16)


def draw_router_grad(key, part):
    return gradient_draw(key, REPLICAS, EXPERTS, WIDTH).astype(jnp.bfloat16)


def steps_of(rng, dims, pieces, smallest, top_value):
    loudness = 1.0
    for position, shards_of in pieces:
        draws = jax.random.uniform(jax.random.fold_in(jax.random.fold_in(rng, 6), position), (shards_of,), jnp.float32, smallest / len(pieces), top_value / len(pieces))
        loudness = loudness * jnp.repeat(jnp.exp(draws), dims[position] // shards_of).reshape((-1,) + (1,) * (len(dims) - 1 - position))
    return loudness


def normal_values(own_key, shape, deviation, most, cuts=(), held_as=jnp.bfloat16):
    result = jax.random.normal(own_key, shape, jnp.float32) * deviation
    if len(cuts) > 0:
        result = steps_of(own_key, shape, cuts, -0.22, 0.18) * result
    return jnp.clip(result, min=-most, max=most).astype(held_as)


def setup_inputs(seed: int = 0) -> dict:
    streams_of = jax.random.split(jax.random.key(seed), 14)
    return {
        "key_grad": draw_key_grad(jax.random.fold_in(streams_of[13], 71), 0),
        "key_error": normal_values(streams_of[1], (REPLICAS, KEY_ROWS, WIDTH), 0.3, 4.0, ((0, 128), (1, 4)), jnp.float32),
        "router_grad": draw_router_grad(jax.random.fold_in(streams_of[13], 71), 0),
        "router_error": normal_values(streams_of[3], (REPLICAS, EXPERTS, WIDTH), 0.3, 4.0, ((0, 128), (1, 4)), jnp.float32),
        "norm_grad": normal_values(streams_of[4], (REPLICAS, NORM_VECS, WIDTH), 2.0, 8.0, ((0, 128), (2, 4))),
        "key_basis": normal_values(streams_of[5], (FACTOR_RANK, WIDTH), 1.0, 6.0, (), jnp.float32),
        "router_basis": normal_values(streams_of[6], (FACTOR_RANK, WIDTH), 1.0, 6.0, (), jnp.float32),
        "key_momentum": normal_values(streams_of[7], (KEY_ROWS, WIDTH), 0.3, 4.0, ((0, 4), (1, 128)), jnp.float32),
        "key_weight": normal_values(streams_of[8], (KEY_ROWS, WIDTH), 0.3, 4.0, ((0, 4), (1, 128)), jnp.float32),
        "router_momentum": normal_values(streams_of[9], (EXPERTS, WIDTH), 0.3, 4.0, ((0, 4), (1, 128)), jnp.float32),
        "router_weight": normal_values(streams_of[10], (EXPERTS, WIDTH), 0.3, 4.0, ((0, 4), (1, 128)), jnp.float32),
        "norm_momentum": normal_values(streams_of[11], (NORM_VECS, WIDTH), 0.3, 4.0, ((1, 4),), jnp.float32),
        "norm_weight": jnp.clip(1.0 + 0.1 * jax.random.normal(streams_of[12], (NORM_VECS, WIDTH), jnp.float32), 0.5, 1.5),
    }


highest = lax.Precision.HIGHEST
momentum_decay = 0.9
learning_rate = 0.1

def inverse_root(gram_matrix):
    scaling = jnp.sqrt(jnp.sum(gram_matrix * gram_matrix)) + 1e-06
    identity = jnp.eye(gram_matrix.shape[0], dtype=jnp.float32)
    square_side = gram_matrix / scaling
    root_side = identity
    for sweep_index in range(ROOT_STEPS):
        middle = 1.5 * identity - 0.5 * jnp.dot(root_side, square_side, precision=highest)
        square_side = jnp.dot(square_side, middle, precision=highest)
        root_side = jnp.dot(middle, root_side, precision=highest)
    return (root_side, scaling)

def compress(gradient, residue, old_basis):
    merged = gradient.astype(jnp.float32) + residue
    summed = lax.optimization_barrier(jnp.sum(merged, axis=0))
    factor_rows = lax.dot_general(old_basis, summed, (((1,), (1,)), ((), ())), precision=highest)
    gram_matrix = lax.dot_general(factor_rows, factor_rows, (((1,), (1,)), ((), ())), precision=highest)
    root_side, scaling = inverse_root(gram_matrix)
    orthonormal = jnp.dot(root_side, factor_rows, precision=highest) / jnp.sqrt(scaling)
    columns = lax.dot_general(summed, orthonormal, (((0,), (1,)), ((), ())), precision=highest) / N_DP
    approx = lax.dot_general(orthonormal, columns, (((0,), (1,)), ((), ())), precision=highest)
    return (merged - approx[None], approx)

def advance(momentum, weight, direction):
    velocity = momentum_decay * momentum + direction
    master = weight - learning_rate * velocity
    return (velocity, master, master.astype(jnp.bfloat16))

def reference(key_grad, key_error, router_grad, router_error, norm_grad, key_basis, router_basis, key_momentum, key_weight, router_momentum, router_weight, norm_momentum, norm_weight):
    key_carry, approx_key = compress(key_grad, key_error, key_basis)
    router_carry, approx_router = compress(router_grad, router_error, router_basis)
    norm_mean = lax.optimization_barrier(jnp.sum(norm_grad.astype(jnp.float32), axis=0)) / N_DP
    key_velocity, key_master, key_params = advance(key_momentum, key_weight, approx_key)
    router_velocity, router_master, router_params = advance(router_momentum, router_weight, approx_router)
    norm_velocity, norm_master, norm_params = advance(norm_momentum, norm_weight, norm_mean)
    return (key_carry, router_carry, key_velocity, key_master, key_params, router_velocity, router_master, router_params, norm_velocity, norm_master, norm_params)
```

```python
import jax
import jax.numpy as jnp
from jax import lax
from jax.sharding import Mesh, PartitionSpec as P

ROOT_STEPS = 4

highest = lax.Precision.HIGHEST
momentum_decay = 0.9
learning_rate = 0.1
f32 = jnp.float32
bf16 = jnp.bfloat16

DP = ("z", "y", "c")
PLANE = ("y", "c", "shard")
LANES = 128
PACK_ROWS = 48


def inverse_root(gram_matrix):
    scaling = jnp.sqrt(jnp.sum(gram_matrix * gram_matrix, axis=(1, 2), keepdims=True)) + 1e-06
    identity = jnp.eye(gram_matrix.shape[1], dtype=f32)[None]
    square_side = gram_matrix / scaling
    root_side = jnp.broadcast_to(identity, gram_matrix.shape)
    for sweep_index in range(ROOT_STEPS):
        middle = 1.5 * identity - 0.5 * batched(root_side, square_side)
        square_side = batched(square_side, middle)
        root_side = batched(middle, root_side)
    return root_side, scaling


def batched(left, right):
    return lax.dot_general(left, right, (((2,), (1,)), ((0,), (0,))), precision=highest)


def dot(left, right, left_dim, right_dim):
    return lax.dot_general(left, right, (((left_dim,), (right_dim,)), ((), ())), precision=highest)


def to_all(block, axes, size):
    spread = jnp.broadcast_to(block[None], (size,) + block.shape)
    return lax.all_to_all(spread, axes, 0, 0, tiled=True)


def body(
    key_grad,
    key_error,
    router_grad,
    router_error,
    norm_grad,
    key_basis,
    router_basis,
    key_momentum,
    key_weight,
    router_momentum,
    router_weight,
    norm_momentum,
    norm_weight,
):
    n_z, n_y, n_c, n_x = (lax.axis_size(name) for name in DP + ("shard",))
    plane = n_y * n_c * n_x
    replicas = n_z * n_y * n_c
    rank_size, width = key_basis.shape
    key_rows, router_rows = key_grad.shape[1], router_grad.shape[1]
    norm_vecs, norm_width = norm_grad.shape[1:]
    col_width = key_momentum.shape[1]
    half = PACK_ROWS // n_c

    decayed_key = key_weight - (learning_rate * momentum_decay) * key_momentum
    decayed_router = router_weight - (learning_rate * momentum_decay) * router_momentum
    decayed_norm = norm_weight - (learning_rate * momentum_decay) * norm_momentum
    norm_lines = norm_vecs * norm_width // LANES
    decayed = jnp.concatenate(
        [
            decayed_key.T,
            jnp.pad(decayed_router.T, ((0, 0), (0, LANES - router_momentum.shape[0]))),
            decayed_norm.reshape(norm_lines, LANES),
        ],
        axis=0,
    )
    decayed = jnp.pad(decayed, ((0, 512 - decayed.shape[0]), (0, 0)))
    decayed, key_error = lax.optimization_barrier((decayed, key_error))
    decayed = lax.all_gather(decayed, "shard", axis=0, tiled=False)

    merged_key = key_grad[0].astype(f32) + key_error[0]
    merged_router = router_grad[0].astype(f32) + router_error[0]
    router_lines = rank_size * router_rows // LANES
    used = rank_size + router_lines + norm_lines
    pack = jnp.concatenate(
        [
            dot(key_basis, merged_key, 1, 1),
            dot(router_basis, merged_router, 1, 1).reshape(router_lines, LANES),
            norm_grad[0].astype(f32).reshape(norm_lines, LANES),
            jnp.zeros((PACK_ROWS - used, LANES), f32),
        ],
        axis=0,
    )
    pair = lax.all_gather(pack, "c", axis=0, tiled=False)
    mine = jnp.sum(lax.dynamic_slice_in_dim(pair, lax.axis_index("c") * half, half, 1), axis=0)
    mine = jnp.sum(to_all(mine, "z", n_z), axis=0)
    spread = to_all(mine, PLANE, plane).reshape(n_y, n_c, n_x, half, LANES)
    full = jnp.sum(spread, axis=0).transpose(1, 0, 2, 3).reshape(n_x, PACK_ROWS, LANES)
    rows_key = full[:, :rank_size].transpose(1, 0, 2).reshape(rank_size, n_x * LANES)
    rows_router = (
        full[:, rank_size : rank_size + router_lines]
        .reshape(n_x, rank_size, router_rows)
        .transpose(1, 0, 2)
        .reshape(rank_size, n_x * router_rows)
    )
    norm_sum = full[:, rank_size + router_lines : used].reshape(n_x, norm_vecs, norm_width)

    grams = jnp.stack([dot(rows_key, rows_key, 1, 1), dot(rows_router, rows_router, 1, 1)])
    roots, scalings = inverse_root(grams)
    ortho_key = dot(roots[0], rows_key, 1, 0) / jnp.sqrt(scalings[0])
    ortho_router = dot(roots[1], rows_router, 1, 0) / jnp.sqrt(scalings[1])
    shard = lax.axis_index("shard")
    own_key = lax.dynamic_slice_in_dim(ortho_key, shard * key_rows, key_rows, 1)
    own_router = lax.dynamic_slice_in_dim(ortho_router, shard * router_rows, router_rows, 1)

    part = jnp.concatenate([dot(own_key, merged_key, 1, 0), dot(own_router, merged_router, 1, 0)])
    groups, lane_groups = 2 * rank_size // 8, plane // (2 * rank_size // 8)
    part = part.astype(bf16).reshape(groups, 8, lane_groups, width // lane_groups)
    part = part.transpose(0, 2, 1, 3).reshape(plane, 8, width // lane_groups)
    part = lax.all_to_all(part, PLANE, 0, 0, tiled=True)
    mine = jnp.sum(part.astype(f32), axis=0).astype(bf16)
    mine = jnp.sum(to_all(mine, "z", n_z).astype(f32), axis=0) / replicas
    columns = to_all(mine.astype(bf16), PLANE, plane)
    columns = columns.reshape(groups, lane_groups, 8, width // lane_groups)
    columns = columns.transpose(0, 2, 1, 3).reshape(2 * rank_size, width).astype(f32)

    key_carry = (merged_key - dot(own_key, columns[:rank_size], 0, 0))[None]
    router_carry = (merged_router - dot(own_router, columns[rank_size:], 0, 0))[None]

    offset = lax.axis_index(DP) * col_width
    few = lax.dynamic_slice_in_dim(columns, offset, col_width, 1)
    approx_key = dot(ortho_key, few[:rank_size], 0, 0)
    approx_router = dot(ortho_router, few[rank_size:], 0, 0)
    norm_mean = norm_sum / replicas

    def advance(momentum, weight, direction):
        velocity = momentum_decay * momentum + direction
        return velocity, weight - learning_rate * velocity

    key_velocity, key_master = advance(
        key_momentum, key_weight, lax.dynamic_slice_in_dim(approx_key, shard * key_rows, key_rows, 0)
    )
    router_velocity, router_master = advance(
        router_momentum,
        router_weight,
        lax.dynamic_slice_in_dim(approx_router, shard * router_rows, router_rows, 0),
    )
    norm_velocity, norm_master = advance(
        norm_momentum, norm_weight, lax.dynamic_index_in_dim(norm_mean, shard, 0, keepdims=False)
    )

    all_key = decayed[:, :col_width].transpose(0, 2, 1).reshape(n_x * key_rows, col_width)
    all_router = decayed[:, col_width : 2 * col_width, :router_rows]
    all_router = all_router.transpose(0, 2, 1).reshape(n_x * router_rows, col_width)
    all_norm = decayed[:, 2 * col_width : 2 * col_width + norm_lines]
    all_norm = all_norm.reshape(n_x, norm_vecs, norm_width)
    key_params = (all_key - learning_rate * approx_key).astype(bf16)
    router_params = (all_router - learning_rate * approx_router).astype(bf16)
    norm_params = (all_norm - learning_rate * norm_mean).astype(bf16)
    norm_params = norm_params.transpose(1, 0, 2).reshape(norm_vecs, n_x * norm_width)
    return (
        key_carry,
        router_carry,
        key_velocity,
        key_master,
        key_params,
        router_velocity,
        router_master,
        router_params,
        norm_velocity,
        norm_master,
        norm_params,
    )


def solution(mesh):
    n_dp, n_x = mesh.devices.shape
    fine = Mesh(mesh.devices.reshape(n_dp // 8, 4, 2, n_x), DP + ("shard",))
    return jax.shard_map(
        body,
        mesh=fine,
        in_specs=(
            P(DP, "shard", None),
            P(DP, "shard", None),
            P(DP, "shard", None),
            P(DP, "shard", None),
            P(DP, None, "shard"),
            P(),
            P(),
            P("shard", DP),
            P("shard", DP),
            P("shard", DP),
            P("shard", DP),
            P(None, "shard"),
            P(None, "shard"),
        ),
        out_specs=(
            P(DP, "shard", None),
            P(DP, "shard", None),
            P("shard", DP),
            P("shard", DP),
            P(None, DP),
            P("shard", DP),
            P("shard", DP),
            P(None, DP),
            P(None, "shard"),
            P(None, "shard"),
            P(),
        ),
        check_vma=False,
    )
```

```python
import jax
import jax.numpy as jnp
from jax import lax
from jax.sharding import Mesh, PartitionSpec as P

ROOT_STEPS = 4

highest = lax.Precision.HIGHEST
momentum_decay = 0.9
learning_rate = 0.1
f32 = jnp.float32
bf16 = jnp.bfloat16

DP = ("z", "y", "c")
PAIRS = ("y", "c")
PLANE = ("y", "c", "shard")
LANES = 128
PACK_ROWS = 64


def inverse_root(gram_matrix):
    scaling = jnp.sqrt(jnp.sum(gram_matrix * gram_matrix, axis=(1, 2), keepdims=True)) + 1e-06
    identity = jnp.eye(gram_matrix.shape[1], dtype=f32)[None]
    square_side = gram_matrix / scaling
    root_side = jnp.broadcast_to(identity, gram_matrix.shape)
    for sweep_index in range(ROOT_STEPS):
        middle = 1.5 * identity - 0.5 * batched(root_side, square_side)
        square_side = batched(square_side, middle)
        root_side = batched(middle, root_side)
    return root_side, scaling


def batched(left, right):
    return lax.dot_general(left, right, (((2,), (1,)), ((0,), (0,))), precision=highest)


def dot(left, right, left_dim, right_dim):
    return lax.dot_general(left, right, (((left_dim,), (right_dim,)), ((), ())), precision=highest)


def to_all(block, axes, size):
    spread = jnp.broadcast_to(block[None], (size,) + block.shape)
    return lax.all_to_all(spread, axes, 0, 0, tiled=True)


def body(
    key_grad,
    key_error,
    router_grad,
    router_error,
    norm_grad,
    key_basis,
    router_basis,
    key_momentum,
    key_weight,
    router_momentum,
    router_weight,
    norm_momentum,
    norm_weight,
):
    n_z, n_y, n_c, n_x = (lax.axis_size(name) for name in DP + ("shard",))
    plane = n_y * n_c * n_x
    replicas = n_z * n_y * n_c
    rank_size, width = key_basis.shape
    key_rows, router_rows = key_grad.shape[1], router_grad.shape[1]
    norm_vecs, norm_width = norm_grad.shape[1:]
    col_width = key_momentum.shape[1]

    decayed_key = key_weight - (learning_rate * momentum_decay) * key_momentum
    decayed_router = router_weight - (learning_rate * momentum_decay) * router_momentum
    decayed_norm = norm_weight - (learning_rate * momentum_decay) * norm_momentum
    norm_lines = norm_vecs * norm_width // LANES
    decayed = jnp.concatenate(
        [
            decayed_key.T,
            jnp.pad(decayed_router.T, ((0, 0), (0, LANES - router_momentum.shape[0]))),
            decayed_norm.reshape(norm_lines, LANES),
        ],
        axis=0,
    )
    near = lax.ppermute(decayed, "shard", [(i, i ^ 1) for i in range(n_x)])
    far = lax.ppermute(decayed, "shard", [(i, i ^ 2) for i in range(n_x)])
    last = lax.ppermute(decayed, "shard", [(i, i ^ 3) for i in range(n_x)])
    by_distance = jnp.stack([decayed, near, far, last])

    merged_key = key_grad[0].astype(f32) + key_error[0]
    merged_router = router_grad[0].astype(f32) + router_error[0]
    router_end = rank_size + router_rows
    used = router_end + norm_lines
    pack = jnp.concatenate(
        [
            dot(key_basis, merged_key, 1, 1),
            jnp.pad(dot(merged_router, router_basis, 1, 1), ((0, 0), (0, LANES - rank_size))),
            norm_grad[0].astype(f32).reshape(norm_lines, LANES),
            jnp.zeros((PACK_ROWS - used, LANES), f32),
        ],
        axis=0,
    )
    pack = pack.reshape(n_y * n_c, PACK_ROWS // (n_y * n_c), LANES)
    mine = jnp.sum(lax.all_to_all(pack, PAIRS, 0, 0, tiled=True), axis=0)
    mine = jnp.sum(to_all(mine, "z", n_z), axis=0)
    full = to_all(mine, PLANE, plane).reshape(n_y * n_c, n_x, PACK_ROWS // (n_y * n_c), LANES)
    full, by_distance = lax.optimization_barrier((full, by_distance))
    decayed = jnp.stack([lax.dynamic_index_in_dim(by_distance, lax.axis_index("shard") ^ x, 0, keepdims=False) for x in range(n_x)])
    full = full.transpose(1, 0, 2, 3).reshape(n_x, PACK_ROWS, LANES)
    rows_key = full[:, :rank_size].transpose(1, 0, 2).reshape(rank_size, n_x * LANES)
    rows_router = full[:, rank_size:router_end, :rank_size].reshape(n_x * router_rows, rank_size).T
    norm_sum = full[:, router_end:used].reshape(n_x, norm_vecs, norm_width)

    grams = jnp.stack([dot(rows_key, rows_key, 1, 1), dot(rows_router, rows_router, 1, 1)])
    roots, scalings = inverse_root(grams)
    ortho_key = dot(roots[0], rows_key, 1, 0) / jnp.sqrt(scalings[0])
    ortho_router = dot(roots[1], rows_router, 1, 0) / jnp.sqrt(scalings[1])
    shard = lax.axis_index("shard")
    own_key = lax.dynamic_slice_in_dim(ortho_key, shard * key_rows, key_rows, 1)
    own_router = lax.dynamic_slice_in_dim(ortho_router, shard * router_rows, router_rows, 1)

    part = jnp.concatenate([dot(own_key, merged_key, 1, 0), dot(own_router, merged_router, 1, 0)])
    groups, lane_groups = 2 * rank_size // 8, plane // (2 * rank_size // 8)
    part = part.astype(bf16).reshape(groups, 8, lane_groups, width // lane_groups)
    part = part.transpose(0, 2, 1, 3).reshape(plane, 8, width // lane_groups)
    part = lax.all_to_all(part, PLANE, 0, 0, tiled=True)
    mine = jnp.sum(part.astype(f32), axis=0).astype(bf16)
    mine = jnp.sum(to_all(mine, "z", n_z).astype(f32), axis=0) / replicas
    columns = to_all(mine.astype(bf16), PLANE, plane)
    columns = columns.reshape(groups, lane_groups, 8, width // lane_groups)
    columns = columns.transpose(0, 2, 1, 3).reshape(2 * rank_size, width).astype(f32)

    key_carry = (merged_key - dot(own_key, columns[:rank_size], 0, 0))[None]
    router_carry = (merged_router - dot(own_router, columns[rank_size:], 0, 0))[None]

    offset = lax.axis_index(DP) * col_width
    few = lax.dynamic_slice_in_dim(columns, offset, col_width, 1)
    approx_key = dot(ortho_key, few[:rank_size], 0, 0)
    approx_router = dot(ortho_router, few[rank_size:], 0, 0)
    norm_mean = norm_sum / replicas

    def advance(momentum, weight, direction):
        velocity = momentum_decay * momentum + direction
        return velocity, weight - learning_rate * velocity

    key_velocity, key_master = advance(
        key_momentum, key_weight, lax.dynamic_slice_in_dim(approx_key, shard * key_rows, key_rows, 0)
    )
    router_velocity, router_master = advance(
        router_momentum,
        router_weight,
        lax.dynamic_slice_in_dim(approx_router, shard * router_rows, router_rows, 0),
    )
    norm_velocity, norm_master = advance(
        norm_momentum, norm_weight, lax.dynamic_index_in_dim(norm_mean, shard, 0, keepdims=False)
    )

    all_key = decayed[:, :col_width].transpose(0, 2, 1).reshape(n_x * key_rows, col_width)
    all_router = decayed[:, col_width : 2 * col_width, :router_rows]
    all_router = all_router.transpose(0, 2, 1).reshape(n_x * router_rows, col_width)
    all_norm = decayed[:, 2 * col_width : 2 * col_width + norm_lines]
    all_norm = all_norm.reshape(n_x, norm_vecs, norm_width)
    key_params = (all_key - learning_rate * approx_key).astype(bf16)
    router_params = (all_router - learning_rate * approx_router).astype(bf16)
    norm_params = (all_norm - learning_rate * norm_mean).astype(bf16)
    norm_params = norm_params.transpose(1, 0, 2).reshape(norm_vecs, n_x * norm_width)
    return (
        key_carry,
        router_carry,
        key_velocity,
        key_master,
        key_params,
        router_velocity,
        router_master,
        router_params,
        norm_velocity,
        norm_master,
        norm_params,
    )


def solution(mesh):
    n_dp, n_x = mesh.devices.shape
    fine = Mesh(mesh.devices.reshape(n_dp // 8, 4, 2, n_x), DP + ("shard",))
    return jax.shard_map(
        body,
        mesh=fine,
        in_specs=(
            P(DP, "shard", None),
            P(DP, "shard", None),
            P(DP, "shard", None),
            P(DP, "shard", None),
            P(DP, None, "shard"),
            P(),
            P(),
            P("shard", DP),
            P("shard", DP),
            P("shard", DP),
            P("shard", DP),
            P(None, "shard"),
            P(None, "shard"),
        ),
        out_specs=(
            P(DP, "shard", None),
            P(DP, "shard", None),
            P("shard", DP),
            P("shard", DP),
            P(None, DP),
            P("shard", DP),
            P("shard", DP),
            P(None, DP),
            P(None, "shard"),
            P(None, "shard"),
            P(),
        ),
        check_vma=False,
    )
```

```python
import jax
import jax.numpy as jnp
from jax import lax
from jax.sharding import Mesh, PartitionSpec as P

ROOT_STEPS = 4

highest = lax.Precision.HIGHEST
momentum_decay = 0.9
learning_rate = 0.1
f32 = jnp.float32
bf16 = jnp.bfloat16

DP = ("z", "y", "c")
PAIRS = ("y", "c")
PLANE = ("y", "c", "shard")
LANES = 128
PACK_ROWS = 64


def inverse_root(gram_matrix):
    scaling = jnp.sqrt(jnp.sum(gram_matrix * gram_matrix, axis=(1, 2), keepdims=True)) + 1e-06
    identity = jnp.eye(gram_matrix.shape[1], dtype=f32)[None]
    square_side = gram_matrix / scaling
    root_side = jnp.broadcast_to(identity, gram_matrix.shape)
    for sweep_index in range(ROOT_STEPS):
        middle = 1.5 * identity - 0.5 * batched(root_side, square_side)
        square_side = batched(square_side, middle)
        root_side = batched(middle, root_side)
    return root_side, scaling


def batched(left, right):
    return lax.dot_general(left, right, (((2,), (1,)), ((0,), (0,))), precision=highest)


def dot(left, right, left_dim, right_dim):
    return lax.dot_general(left, right, (((left_dim,), (right_dim,)), ((), ())), precision=highest)


def to_all(block, axes, size):
    spread = jnp.broadcast_to(block[None], (size,) + block.shape)
    return lax.all_to_all(spread, axes, 0, 0, tiled=True)


def body(
    key_grad,
    key_error,
    router_grad,
    router_error,
    norm_grad,
    key_basis,
    router_basis,
    key_momentum,
    key_weight,
    router_momentum,
    router_weight,
    norm_momentum,
    norm_weight,
):
    n_z, n_y, n_c, n_x = (lax.axis_size(name) for name in DP + ("shard",))
    plane = n_y * n_c * n_x
    replicas = n_z * n_y * n_c
    rank_size, width = key_basis.shape
    key_rows, router_rows = key_grad.shape[1], router_grad.shape[1]
    norm_vecs, norm_width = norm_grad.shape[1:]
    col_width = key_momentum.shape[1]

    decayed_key = key_weight - (learning_rate * momentum_decay) * key_momentum
    decayed_router = router_weight - (learning_rate * momentum_decay) * router_momentum
    decayed_norm = norm_weight - (learning_rate * momentum_decay) * norm_momentum
    norm_lines = norm_vecs * norm_width // LANES
    decayed = jnp.concatenate(
        [
            decayed_key.T,
            jnp.pad(decayed_router.T, ((0, 0), (0, LANES - router_momentum.shape[0]))),
            decayed_norm.reshape(norm_lines, LANES),
        ],
        axis=0,
    )
    merged_key = key_grad[0].astype(f32) + key_error[0]
    merged_router = router_grad[0].astype(f32) + router_error[0]
    router_end = rank_size + router_rows
    used = router_end + norm_lines
    pack = jnp.concatenate(
        [
            dot(key_basis, merged_key, 1, 1),
            jnp.pad(dot(merged_router, router_basis, 1, 1), ((0, 0), (0, LANES - rank_size))),
            norm_grad[0].astype(f32).reshape(norm_lines, LANES),
            jnp.zeros((PACK_ROWS - used, LANES), f32),
        ],
        axis=0,
    )
    pair = lax.all_gather(pack, "c", axis=0, tiled=False)
    half = PACK_ROWS // n_c
    mine = jnp.sum(lax.dynamic_slice_in_dim(pair, lax.axis_index("c") * half, half, 1), axis=0)
    mine = jnp.sum(to_all(mine.astype(bf16), "z", n_z).astype(f32), axis=0)
    spread = to_all(mine, PAIRS, n_y * n_c).reshape(n_y, n_c, half, LANES)
    own = jnp.sum(spread, axis=0).reshape(PACK_ROWS, LANES)

    part = jnp.concatenate(
        [
            dot(own[:rank_size], merged_key, 1, 0),
            dot(own[rank_size:router_end, :rank_size], merged_router, 0, 0),
        ]
    )
    groups, lane_groups = 2 * rank_size // 8, plane // (2 * rank_size // 8)
    part = part.astype(bf16).reshape(groups, 8, lane_groups, width // lane_groups)
    part = part.transpose(0, 2, 1, 3).reshape(plane, 8, width // lane_groups)
    sent = jnp.concatenate([own, decayed])
    near = lax.ppermute(sent, "shard", [(i, i ^ 1) for i in range(n_x)])
    far = lax.ppermute(sent, "shard", [(i, i ^ 2) for i in range(n_x)])
    last = lax.ppermute(sent, "shard", [(i, i ^ 3) for i in range(n_x)])
    part = lax.all_to_all(part, PLANE, 0, 0, tiled=True)
    mine = jnp.sum(part.astype(f32), axis=0).astype(bf16)
    mine, near, far, last = lax.optimization_barrier((mine, near, far, last))
    by_distance = jnp.stack([sent, near, far, last])
    some_key = by_distance[:, :rank_size]
    some_router = by_distance[:, rank_size:router_end, :rank_size]
    grams = jnp.stack(
        [
            lax.dot_general(some_key, some_key, (((0, 2), (0, 2)), ((), ())), precision=highest),
            lax.dot_general(some_router, some_router, (((0, 1), (0, 1)), ((), ())), precision=highest),
        ]
    )
    roots, scalings = inverse_root(grams)
    squares = lax.dot_general(roots, roots, (((1,), (1,)), ((0,), (0,))), precision=highest)
    squares = squares / (scalings * replicas)
    shard = lax.axis_index("shard")
    by_shard = jnp.stack(
        [lax.dynamic_index_in_dim(by_distance, shard ^ x, 0, keepdims=False) for x in range(n_x)]
    )
    mine = jnp.sum(to_all(mine, "z", n_z).astype(f32), axis=0).astype(bf16)
    mine, squares, by_shard = lax.optimization_barrier((mine, squares, by_shard))
    sums = to_all(mine, PLANE, plane)
    sums = sums.reshape(groups, lane_groups, 8, width // lane_groups)
    sums = sums.transpose(0, 2, 1, 3).reshape(2 * rank_size, width).astype(f32)

    rows_key = by_shard[:, :rank_size].transpose(1, 0, 2).reshape(rank_size, n_x * LANES)
    rows_router = by_shard[:, rank_size:router_end, :rank_size].reshape(n_x * router_rows, rank_size)
    norm_sum = by_shard[:, router_end:used].reshape(n_x, norm_vecs, norm_width)
    decayed = by_shard[:, PACK_ROWS:]

    left_key = dot(own[:rank_size], squares[0], 0, 0)
    left_router = dot(own[rank_size:router_end, :rank_size], squares[1], 1, 0)
    key_carry = (merged_key - dot(left_key, sums[:rank_size], 1, 0))[None]
    router_carry = (merged_router - dot(left_router, sums[rank_size:], 1, 0))[None]

    offset = lax.axis_index(DP) * col_width
    few = lax.dynamic_slice_in_dim(sums, offset, col_width, 1)
    approx_key = dot(rows_key, dot(squares[0], few[:rank_size], 1, 0), 0, 0)
    approx_router = dot(rows_router, dot(squares[1], few[rank_size:], 1, 0), 1, 0)
    norm_mean = norm_sum / replicas

    def advance(momentum, weight, direction):
        velocity = momentum_decay * momentum + direction
        return velocity, weight - learning_rate * velocity

    key_velocity, key_master = advance(
        key_momentum, key_weight, lax.dynamic_slice_in_dim(approx_key, shard * key_rows, key_rows, 0)
    )
    router_velocity, router_master = advance(
        router_momentum,
        router_weight,
        lax.dynamic_slice_in_dim(approx_router, shard * router_rows, router_rows, 0),
    )
    norm_velocity, norm_master = advance(
        norm_momentum, norm_weight, lax.dynamic_index_in_dim(norm_mean, shard, 0, keepdims=False)
    )

    all_key = decayed[:, :col_width].transpose(0, 2, 1).reshape(n_x * key_rows, col_width)
    all_router = decayed[:, col_width : 2 * col_width, :router_rows]
    all_router = all_router.transpose(0, 2, 1).reshape(n_x * router_rows, col_width)
    all_norm = decayed[:, 2 * col_width : 2 * col_width + norm_lines]
    all_norm = all_norm.reshape(n_x, norm_vecs, norm_width)
    key_params = (all_key - learning_rate * approx_key).astype(bf16)
    router_params = (all_router - learning_rate * approx_router).astype(bf16)
    norm_params = (all_norm - learning_rate * norm_mean).astype(bf16)
    norm_params = norm_params.transpose(1, 0, 2).reshape(norm_vecs, n_x * norm_width)
    return (
        key_carry,
        router_carry,
        key_velocity,
        key_master,
        key_params,
        router_velocity,
        router_master,
        router_params,
        norm_velocity,
        norm_master,
        norm_params,
    )


def solution(mesh):
    n_dp, n_x = mesh.devices.shape
    fine = Mesh(mesh.devices.reshape(n_dp // 8, 4, 2, n_x), DP + ("shard",))
    return jax.shard_map(
        body,
        mesh=fine,
        in_specs=(
            P(DP, "shard", None),
            P(DP, "shard", None),
            P(DP, "shard", None),
            P(DP, "shard", None),
            P(DP, None, "shard"),
            P(),
            P(),
            P("shard", DP),
            P("shard", DP),
            P("shard", DP),
            P("shard", DP),
            P(None, "shard"),
            P(None, "shard"),
        ),
        out_specs=(
            P(DP, "shard", None),
            P(DP, "shard", None),
            P("shard", DP),
            P("shard", DP),
            P(None, DP),
            P("shard", DP),
            P("shard", DP),
            P(None, DP),
            P(None, "shard"),
            P(None, "shard"),
            P(),
        ),
        check_vma=False,
    )
```

```python
import jax
import jax.numpy as jnp
from jax import lax
from jax.experimental import pallas as pl
from jax.experimental.pallas import tpu as pltpu
from jax.sharding import Mesh, PartitionSpec as P

ROOT_STEPS = 4

highest = lax.Precision.HIGHEST
momentum_decay = 0.9
learning_rate = 0.1
f32 = jnp.float32
bf16 = jnp.bfloat16

DP = ("z", "y", "c")
PAIRS = ("y", "c")
PLANE = ("y", "c", "shard")
LANES = 128
PACK_ROWS = 64
KEY_AT, ROUTER_AT, NORM_AT = 64, 88, 104


def dot(left, right, left_dim, right_dim):
    return lax.dot_general(left, right, (((left_dim,), (right_dim,)), ((), ())), precision=highest)


def in_vmem(array):
    return pltpu.with_memory_space_constraint(array, pltpu.VMEM)


def head_kernel(kb_ref, rb_ref, kg_ref, ke_ref, rg_ref, re_ref, ng_ref, out_ref):
    rank_size, router_rows = kb_ref.shape[0], rg_ref.shape[1]
    norm_vecs, norm_width = ng_ref.shape[1:]
    router_end = rank_size + router_rows

    @pl.when(pl.program_id(0) == 0)
    def _():
        out_ref[...] = jnp.zeros_like(out_ref)
        norm = ng_ref[0].astype(f32)
        lines = norm_width // LANES
        for vec in range(norm_vecs):
            for line in range(lines):
                row = router_end + vec * lines + line
                out_ref[row : row + 1, :] = norm[vec : vec + 1, line * LANES : (line + 1) * LANES]

    merged_key = kg_ref[0].astype(f32) + ke_ref[0]
    merged_router = rg_ref[0].astype(f32) + re_ref[0]
    out_ref[:rank_size, :] += dot(kb_ref[...], merged_key, 1, 1)
    out_ref[rank_size:router_end, :rank_size] += dot(merged_router, rb_ref[...], 1, 1)


def head(key_basis, router_basis, key_grad, key_error, router_grad, router_error, norm_grad):
    rank_size, width = key_basis.shape
    key_rows, router_rows = key_grad.shape[1], router_grad.shape[1]
    steps = 5
    block = width // steps
    return pl.pallas_call(
        head_kernel,
        grid=(steps,),
        in_specs=[
            pl.BlockSpec((rank_size, block), lambda i: (0, i)),
            pl.BlockSpec((rank_size, block), lambda i: (0, i)),
            pl.BlockSpec((1, key_rows, block), lambda i: (0, 0, i)),
            pl.BlockSpec((1, key_rows, block), lambda i: (0, 0, i)),
            pl.BlockSpec((1, router_rows, block), lambda i: (0, 0, i)),
            pl.BlockSpec((1, router_rows, block), lambda i: (0, 0, i)),
            pl.BlockSpec(norm_grad.shape, lambda i: (0, 0, 0)),
        ],
        out_specs=pl.BlockSpec((PACK_ROWS, LANES), lambda i: (0, 0)),
        out_shape=jax.ShapeDtypeStruct((PACK_ROWS, LANES), f32),
        name="head",
    )(key_basis, router_basis, key_grad, key_error, router_grad, router_error, norm_grad)


def square_of_root(gram, replicas):
    scaling = jnp.sqrt(jnp.sum(gram * gram, axis=(0, 1), keepdims=True)) + 1e-06
    rows = lax.broadcasted_iota(jnp.int32, gram.shape, 0)
    identity = (rows == lax.broadcasted_iota(jnp.int32, gram.shape, 1)).astype(f32)
    square_side, root_side = gram / scaling, identity
    for sweep_index in range(ROOT_STEPS):
        middle = 1.5 * identity - 0.5 * dot(root_side, square_side, 1, 0)
        square_side = dot(square_side, middle, 1, 0)
        root_side = dot(middle, root_side, 1, 0)
    return dot(root_side, root_side, 0, 0) / (scaling * replicas)


def side_kernel(replicas, rank_size, router_rows, col_width, *refs):
    packs = [ref.at[i] for ref in refs[:2] for i in range(2)]
    outs = refs[2:]
    lk_ref, lt_ref, lr_ref, dk_ref, dr_ref, ns_ref, dn_ref = outs
    router_end = rank_size + router_rows
    shard = lax.axis_index("shard")
    key_rows = [pack[:rank_size, :] for pack in packs]
    rout_rows = [pack[rank_size:router_end, :rank_size] for pack in packs]
    square_key = square_of_root(sum(dot(rows, rows, 1, 1) for rows in key_rows), replicas)
    square_router = square_of_root(sum(dot(rows, rows, 0, 0) for rows in rout_rows), replicas)
    lk_ref[...] = dot(key_rows[0], square_key, 0, 0)
    for distance, pack in enumerate(packs):
        place = lax.bitwise_xor(shard, distance)
        lanes = pl.ds(pl.multiple_of(place * LANES, LANES), LANES)
        lines = pl.ds(pl.multiple_of(place * router_rows, router_rows), router_rows)
        lt_ref[:, lanes] = dot(square_key, key_rows[distance], 0, 0)
        lr_ref[lines, :] = dot(rout_rows[distance], square_router, 1, 0)
        dk_ref[:, lanes] = pack[KEY_AT : KEY_AT + col_width, :]
        dr_ref[lines, :] = pack[ROUTER_AT : ROUTER_AT + router_rows, :]
        ns_ref[place] = pack[router_end : router_end + 16, :]
        dn_ref[place] = pack[NORM_AT : NORM_AT + 16, :]


def side(packs, replicas, rank_size, router_rows, col_width):
    n_x = 2 * len(packs)
    shapes = [
        (LANES, rank_size),
        (rank_size, n_x * LANES),
        (n_x * router_rows, rank_size),
        (col_width, n_x * LANES),
        (n_x * router_rows, LANES),
        (n_x, 16, LANES),
        (n_x, 16, LANES),
    ]
    return pl.pallas_call(
        lambda *refs: side_kernel(replicas, rank_size, router_rows, col_width, *refs),
        out_shape=[jax.ShapeDtypeStruct(shape, f32) for shape in shapes],
        in_specs=[pl.BlockSpec(memory_space=pltpu.VMEM)] * len(packs),
        out_specs=[pl.BlockSpec(memory_space=pltpu.VMEM)] * len(shapes),
        cost_estimate=pl.CostEstimate(flops=200000000, bytes_accessed=8000000, transcendentals=0),
        name="side",
    )(*[in_vmem(x) for x in packs])


def tail_kernel(
    t_ref, kg_ref, ke_ref, rg_ref, re_ref, lk_ref, lt_ref, lr_ref, dk_ref, dr_ref, km_ref, kw_ref, rm_ref, rw_ref,
    kc_ref, rc_ref, kv_ref, kn_ref, kp_ref, rv_ref, rn_ref, rp_ref,
):
    groups, lane_groups, _, block = t_ref.shape
    rank_size = groups * 4
    half = groups // 2
    router_rows, col_width = rm_ref.shape
    shard = lax.axis_index("shard")
    step = pl.program_id(0)
    own_lines = pl.ds(pl.multiple_of(shard * router_rows, router_rows), router_rows)

    def sums(first, lane_group):
        return jnp.concatenate([t_ref[first + i, lane_group].astype(f32) for i in range(half)], axis=0)

    def apply(left, right):
        high = left.astype(bf16)
        low = (left - high.astype(f32)).astype(bf16)
        terms = [
            lax.dot_general(term, right, (((1,), (0,)), ((), ())), preferred_element_type=f32)
            for term in (high, low)
        ]
        return terms[0] + terms[1]

    key_sums = sums(0, step).astype(bf16)
    router_sums = sums(half, step).astype(bf16)
    cols = pl.ds(pl.multiple_of(step * block, LANES), block)
    kc_ref[0] = kg_ref[0, :, cols].astype(f32) + ke_ref[0, :, cols] - apply(lk_ref[...], key_sums)
    rc_ref[0] = rg_ref[0, :, cols].astype(f32) + re_ref[0, :, cols] - apply(lr_ref[own_lines, :], router_sums)

    @pl.when(step == 0)
    def _():
        place = (lax.axis_index("z") * lax.axis_size("y") + lax.axis_index("y")) * lax.axis_size("c")
        column = (place + lax.axis_index("c")) * col_width
        lane_group = column // block
        offset = column - lane_group * block
        lines = lax.broadcasted_iota(jnp.int32, (block, LANES), 0)
        picks = lines == lax.broadcasted_iota(jnp.int32, (block, LANES), 1) + offset
        picks = picks.astype(f32).astype(bf16)

        def few(first):
            return lax.dot_general(
                sums(first, lane_group).astype(bf16), picks, (((1,), (0,)), ((), ())), preferred_element_type=f32
            )

        few_key, few_router = few(0), few(half)
        approx = dot(few_key, lt_ref[...], 0, 0)[:col_width]
        kp_ref[...] = (dk_ref[...] - learning_rate * approx).astype(bf16)
        own_lanes = pl.ds(pl.multiple_of(shard * LANES, LANES), LANES)
        own = dot(few_key, lt_ref[:, own_lanes], 0, 0)[:col_width]
        velocity = momentum_decay * km_ref[...] + own
        kv_ref[...] = velocity
        kn_ref[...] = kw_ref[...] - learning_rate * velocity
        approx = dr_ref[...] - learning_rate * dot(lr_ref[...], few_router, 1, 0)
        rp_ref[...] = approx.T[:col_width].astype(bf16)
        own = dot(lr_ref[own_lines, :], few_router, 1, 0)[:, :col_width]
        velocity = momentum_decay * rm_ref[...] + own
        rv_ref[...] = velocity
        rn_ref[...] = rw_ref[...] - learning_rate * velocity


def tail(sums, key_grad, key_error, router_grad, router_error, *small):
    lane_groups, block = sums.shape[1], sums.shape[3]
    key_rows, router_rows = key_grad.shape[1], router_grad.shape[1]
    dk, dr, km, rm = small[3], small[4], small[5], small[7]
    wide = [
        pl.BlockSpec((1, key_rows, block), lambda i: (0, 0, i)),
        pl.BlockSpec((1, router_rows, block), lambda i: (0, 0, i)),
    ]

    def whole(shape):
        return pl.BlockSpec(shape, lambda i: (0,) * len(shape))

    outs = [
        (key_grad.shape, f32),
        (router_grad.shape, f32),
        (km.shape, f32),
        (km.shape, f32),
        (dk.shape, bf16),
        (rm.shape, f32),
        (rm.shape, f32),
        ((dk.shape[0], dr.shape[0]), bf16),
    ]
    return pl.pallas_call(
        tail_kernel,
        grid=(lane_groups,),
        in_specs=[pl.BlockSpec(memory_space=pltpu.VMEM)] * (5 + len(small)),
        out_specs=wide + [whole(shape) for shape, _ in outs[2:]],
        out_shape=[jax.ShapeDtypeStruct(shape, dtype) for shape, dtype in outs],
        name="tail",
    )(*[in_vmem(x) for x in (sums, key_grad, key_error, router_grad, router_error) + small])


def to_all(block, axes, size):
    spread = jnp.broadcast_to(block[None], (size,) + block.shape)
    return lax.all_to_all(spread, axes, 0, 0, tiled=True)


def body(
    key_grad,
    key_error,
    router_grad,
    router_error,
    norm_grad,
    key_basis,
    router_basis,
    key_momentum,
    key_weight,
    router_momentum,
    router_weight,
    norm_momentum,
    norm_weight,
):
    n_z, n_y, n_c, n_x = (lax.axis_size(name) for name in DP + ("shard",))
    plane = n_y * n_c * n_x
    replicas = n_z * n_y * n_c
    rank_size, width = key_basis.shape
    key_rows, router_rows = key_grad.shape[1], router_grad.shape[1]
    norm_vecs, norm_width = norm_grad.shape[1:]
    col_width = key_momentum.shape[1]

    decayed_key = key_weight - (learning_rate * momentum_decay) * key_momentum
    decayed_router = router_weight - (learning_rate * momentum_decay) * router_momentum
    decayed_norm = norm_weight - (learning_rate * momentum_decay) * norm_momentum
    norm_lines = norm_vecs * norm_width // LANES
    decayed = jnp.concatenate(
        [
            jnp.pad(decayed_key.T, ((0, ROUTER_AT - KEY_AT - col_width), (0, 0))),
            jnp.pad(decayed_router, ((0, 0), (0, LANES - col_width))),
            jnp.pad(decayed_norm.reshape(norm_lines, LANES), ((0, 16 - norm_lines), (0, 0))),
        ],
        axis=0,
    )

    merged = jnp.concatenate(
        [key_grad[0].astype(f32) + key_error[0], router_grad[0].astype(f32) + router_error[0]]
    )
    router_end = rank_size + router_rows
    used = router_end + norm_lines
    pack = head(key_basis, router_basis, key_grad, key_error, router_grad, router_error, norm_grad)
    pair = lax.all_gather(pack, "c", axis=0, tiled=False)
    half = PACK_ROWS // n_c
    mine = jnp.sum(lax.dynamic_slice_in_dim(pair, lax.axis_index("c") * half, half, 1), axis=0)
    mine = jnp.sum(to_all(mine.astype(bf16), "z", n_z).astype(f32), axis=0)
    spread = to_all(mine, PAIRS, n_y * n_c).reshape(n_y, n_c, half, LANES)
    own = jnp.sum(spread, axis=0).reshape(PACK_ROWS, LANES)

    left = jnp.concatenate(
        [
            jnp.pad(own[:rank_size], ((0, 0), (0, router_rows))),
            jnp.pad(own[rank_size:router_end, :rank_size].T, ((0, 0), (key_rows, 0))),
        ]
    )
    part = lax.dot_general(left, merged, (((1,), (0,)), ((), ())), precision=lax.Precision.HIGH)
    groups, lane_groups = 2 * rank_size // 8, plane // (2 * rank_size // 8)
    part = part.astype(bf16).reshape(groups, 8, lane_groups, width // lane_groups)
    part = part.transpose(0, 2, 1, 3).reshape(plane, 8, width // lane_groups)
    sent = jnp.concatenate([own, decayed])
    near = lax.ppermute(sent, "shard", [(i, i ^ 1) for i in range(n_x)])
    part = lax.all_to_all(part, PLANE, 0, 0, tiled=True)
    mine = jnp.sum(part.astype(f32), axis=0).astype(bf16)
    mine, near = lax.optimization_barrier((mine, near))
    packs = jnp.stack([sent, near])
    far = lax.ppermute(packs, "shard", [(i, i ^ 2) for i in range(n_x)])
    *lefts, norm_sum, decayed_norm = side([packs, far], replicas, rank_size, router_rows, col_width)
    mine = jnp.sum(to_all(mine, "z", n_z).astype(f32), axis=0).astype(bf16)
    mine, lefts, norm_sum, decayed_norm = lax.optimization_barrier((mine, lefts, norm_sum, decayed_norm))
    sums = to_all(mine, PLANE, plane).reshape(groups, lane_groups, 8, width // lane_groups)
    (key_carry, router_carry, key_velocity, key_master, key_params, router_velocity, router_master, router_params) = (
        tail(
            sums,
            key_grad,
            key_error,
            router_grad,
            router_error,
            *lefts,
            key_momentum.T,
            key_weight.T,
            router_momentum,
            router_weight,
        )
    )

    norm_mean = norm_sum[:, :norm_lines].reshape(n_x, norm_vecs, norm_width) / replicas
    shard = lax.axis_index("shard")
    def advance(momentum, weight, direction):
        velocity = momentum_decay * momentum + direction
        return velocity, weight - learning_rate * velocity

    norm_velocity, norm_master = advance(
        norm_momentum, norm_weight, lax.dynamic_index_in_dim(norm_mean, shard, 0, keepdims=False)
    )

    all_norm = decayed_norm[:, :norm_lines].reshape(n_x, norm_vecs, norm_width)
    norm_params = (all_norm - learning_rate * norm_mean).astype(bf16)
    norm_params = norm_params.transpose(1, 0, 2).reshape(norm_vecs, n_x * norm_width)
    return (
        key_carry,
        router_carry,
        key_velocity.T,
        key_master.T,
        key_params.T,
        router_velocity,
        router_master,
        router_params.T,
        norm_velocity,
        norm_master,
        norm_params,
    )


def solution(mesh):
    n_dp, n_x = mesh.devices.shape
    fine = Mesh(mesh.devices.reshape(n_dp // 8, 4, 2, n_x), DP + ("shard",))
    return jax.shard_map(
        body,
        mesh=fine,
        in_specs=(
            P(DP, "shard", None),
            P(DP, "shard", None),
            P(DP, "shard", None),
            P(DP, "shard", None),
            P(DP, None, "shard"),
            P(),
            P(),
            P("shard", DP),
            P("shard", DP),
            P("shard", DP),
            P("shard", DP),
            P(None, "shard"),
            P(None, "shard"),
        ),
        out_specs=(
            P(DP, "shard", None),
            P(DP, "shard", None),
            P("shard", DP),
            P("shard", DP),
            P(None, DP),
            P("shard", DP),
            P("shard", DP),
            P(None, DP),
            P(None, "shard"),
            P(None, "shard"),
            P(),
        ),
        check_vma=False,
    )
```

```python
import jax
import jax.numpy as jnp
from jax import lax
from jax.experimental import pallas as pl
from jax.experimental.pallas import tpu as pltpu
from jax.sharding import Mesh, PartitionSpec as P

ROOT_STEPS = 4

highest = lax.Precision.HIGHEST
momentum_decay = 0.9
learning_rate = 0.1
f32 = jnp.float32
bf16 = jnp.bfloat16

DP = ("z", "y", "c")
PAIRS = ("y", "c")
PLANE = ("y", "c", "shard")
LANES = 128
TAIL_PARTS = 2
PACK_ROWS = 64
KEY_AT, ROUTER_AT, NORM_AT = 64, 88, 104


def dot(left, right, left_dim, right_dim):
    return lax.dot_general(left, right, (((left_dim,), (right_dim,)), ((), ())), precision=highest)


def in_halves(left, right, left_dim, right_dim):
    left_high, right_high = left.astype(bf16), right.astype(bf16)
    left_low = (left - left_high.astype(f32)).astype(bf16)
    right_low = (right - right_high.astype(f32)).astype(bf16)
    total = 0.0
    for one, other in ((left_low, right_high), (left_high, right_low), (left_high, right_high)):
        total = total + lax.dot_general(
            one, other, (((left_dim,), (right_dim,)), ((), ())), preferred_element_type=f32
        )
    return total


def in_vmem(array):
    return pltpu.with_memory_space_constraint(array, pltpu.VMEM)


def head_kernel(kb_ref, rb_ref, kg_ref, ke_ref, rg_ref, re_ref, ng_ref, out_ref):
    rank_size, router_rows = kb_ref.shape[0], rg_ref.shape[1]
    norm_vecs, norm_width = ng_ref.shape[1:]
    router_end = rank_size + router_rows

    @pl.when(pl.program_id(0) == 0)
    def _():
        out_ref[...] = jnp.zeros_like(out_ref)
        norm = ng_ref[0].astype(f32)
        lines = norm_width // LANES
        for vec in range(norm_vecs):
            for line in range(lines):
                row = router_end + vec * lines + line
                out_ref[row : row + 1, :] = norm[vec : vec + 1, line * LANES : (line + 1) * LANES]

    merged_key = kg_ref[0].astype(f32) + ke_ref[0]
    merged_router = rg_ref[0].astype(f32) + re_ref[0]
    out_ref[:rank_size, :] += in_halves(kb_ref[...], merged_key, 1, 1)
    out_ref[rank_size:router_end, :rank_size] += in_halves(merged_router, rb_ref[...], 1, 1)


def head(key_basis, router_basis, key_grad, key_error, router_grad, router_error, norm_grad):
    rank_size, width = key_basis.shape
    key_rows, router_rows = key_grad.shape[1], router_grad.shape[1]
    steps = 2
    block = width // steps
    return pl.pallas_call(
        head_kernel,
        grid=(steps,),
        in_specs=[
            pl.BlockSpec((rank_size, block), lambda i: (0, i)),
            pl.BlockSpec((rank_size, block), lambda i: (0, i)),
            pl.BlockSpec((1, key_rows, block), lambda i: (0, 0, i)),
            pl.BlockSpec((1, key_rows, block), lambda i: (0, 0, i)),
            pl.BlockSpec((1, router_rows, block), lambda i: (0, 0, i)),
            pl.BlockSpec((1, router_rows, block), lambda i: (0, 0, i)),
            pl.BlockSpec(norm_grad.shape, lambda i: (0, 0, 0)),
        ],
        out_specs=pl.BlockSpec((PACK_ROWS, LANES), lambda i: (0, 0)),
        out_shape=jax.ShapeDtypeStruct((PACK_ROWS, LANES), f32),
        name="head",
    )(key_basis, router_basis, key_grad, key_error, router_grad, router_error, norm_grad)


def mid_kernel(
    own_ref, kg_ref, ke_ref, rg_ref, re_ref, km_ref, kw_ref, rm_ref, rw_ref, nm_ref, nw_ref, part_ref, sent_ref
):
    groups, lane_groups, lines, block = part_ref.shape
    half, (router_rows, col_width) = groups // 2, rm_ref.shape
    rank_size = half * lines
    key_rows = own_ref[:rank_size, :]
    rout_rows = own_ref[rank_size : rank_size + router_rows, :rank_size]
    for group in range(lane_groups):
        cols = slice(group * block, (group + 1) * block)
        key_part = in_halves(key_rows, kg_ref[0, :, cols].astype(f32) + ke_ref[0, :, cols], 1, 0)
        rout_part = in_halves(rout_rows, rg_ref[0, :, cols].astype(f32) + re_ref[0, :, cols], 0, 0)
        for i in range(half):
            part_ref[i, group] = key_part[i * lines : (i + 1) * lines].astype(bf16)
            part_ref[half + i, group] = rout_part[i * lines : (i + 1) * lines].astype(bf16)
    decay = learning_rate * momentum_decay
    sent_ref[:KEY_AT, :] = own_ref[...]
    sent_ref[KEY_AT:, :] = jnp.zeros((sent_ref.shape[0] - KEY_AT, LANES), f32)
    sent_ref[KEY_AT : KEY_AT + col_width, :] = kw_ref[...] - decay * km_ref[...]
    sent_ref[ROUTER_AT : ROUTER_AT + router_rows, :col_width] = rw_ref[...] - decay * rm_ref[...]
    norm = nw_ref[...] - decay * nm_ref[...]
    norm_vecs, norm_width = norm.shape
    for vec in range(norm_vecs):
        for first in range(0, norm_width, LANES):
            row = NORM_AT + (vec * norm_width + first) // LANES
            sent_ref[row : row + 1, :] = norm[vec : vec + 1, first : first + LANES]


def mid(chunks, *operands):
    return pl.pallas_call(
        mid_kernel,
        in_specs=[pl.BlockSpec(memory_space=pltpu.VMEM)] * len(operands),
        out_specs=[pl.BlockSpec(chunks, lambda: (0,) * len(chunks)), pl.BlockSpec(memory_space=pltpu.VMEM)],
        out_shape=[jax.ShapeDtypeStruct(chunks, bf16), pltpu.VMEM((NORM_AT + 16, LANES), f32)],
        name="mid",
    )(*[in_vmem(x) for x in operands])


def square_of_root(gram, replicas):
    scaling = jnp.sqrt(jnp.sum(gram * gram, axis=(0, 1), keepdims=True)) + 1e-06
    rows = lax.broadcasted_iota(jnp.int32, gram.shape, 0)
    identity = (rows == lax.broadcasted_iota(jnp.int32, gram.shape, 1)).astype(f32)
    square_side, root_side = gram / scaling, identity
    for sweep_index in range(ROOT_STEPS):
        middle = 1.5 * identity - 0.5 * dot(root_side, square_side, 1, 0)
        square_side = dot(square_side, middle, 1, 0)
        root_side = dot(middle, root_side, 1, 0)
    return dot(root_side, root_side, 0, 0) / (scaling * replicas)


def side_kernel(replicas, rank_size, router_rows, col_width, *refs):
    packs = [ref.at[i] for ref in refs[:2] for i in range(2)]
    nm_ref, nw_ref, lk_ref, lt_ref, lr_ref, dk_ref, dr_ref, nv_ref, nn_ref, np_ref, wide_ref = refs[2:]
    norm_vecs, norm_width = nm_ref.shape
    router_end = rank_size + router_rows
    shard = lax.axis_index("shard")
    key_rows = [pack[:rank_size, :] for pack in packs]
    rout_rows = [pack[rank_size:router_end, :rank_size] for pack in packs]
    square_key = square_of_root(sum(dot(rows, rows, 1, 1) for rows in key_rows), replicas)
    square_router = square_of_root(sum(dot(rows, rows, 0, 0) for rows in rout_rows), replicas)
    lk_ref[...] = dot(key_rows[0], square_key, 0, 0)
    for distance, pack in enumerate(packs):
        place = lax.bitwise_xor(shard, distance)
        lanes = pl.ds(pl.multiple_of(place * LANES, LANES), LANES)
        lines = pl.ds(pl.multiple_of(place * router_rows, router_rows), router_rows)
        lt_ref[:, lanes] = dot(square_key, key_rows[distance], 0, 0)
        lr_ref[lines, :] = dot(rout_rows[distance], square_router, 1, 0)
        dk_ref[:, lanes] = pack[KEY_AT : KEY_AT + col_width, :]
        dr_ref[lines, :] = pack[ROUTER_AT : ROUTER_AT + router_rows, :]
        for vec in range(norm_vecs):
            for first in range(0, norm_width, LANES):
                line = (vec * norm_width + first) // LANES
                mean = pack[router_end + line : router_end + line + 1, :] / replicas
                master = pack[NORM_AT + line : NORM_AT + line + 1, :] - learning_rate * mean
                lanes = pl.ds(pl.multiple_of(place * norm_width + first, LANES), LANES)
                wide_ref[vec : vec + 1, lanes] = master
                if distance == 0:
                    here = slice(first, first + LANES)
                    velocity = momentum_decay * nm_ref[vec : vec + 1, here] + mean
                    nv_ref[vec : vec + 1, here] = velocity
                    nn_ref[vec : vec + 1, here] = nw_ref[vec : vec + 1, here] - learning_rate * velocity
    np_ref[...] = wide_ref[...].astype(bf16)


def side(packs, norm_state, replicas, rank_size, router_rows, col_width):
    n_x = 2 * len(packs)
    shapes = [
        (LANES, rank_size),
        (rank_size, n_x * LANES),
        (n_x * router_rows, rank_size),
        (col_width, n_x * LANES),
        (n_x * router_rows, LANES),
    ]
    norm_vecs, norm_width = norm_state[0].shape
    norms = [((norm_vecs, norm_width), f32)] * 2 + [((norm_vecs, n_x * norm_width), bf16)]
    return pl.pallas_call(
        lambda *refs: side_kernel(replicas, rank_size, router_rows, col_width, *refs),
        out_shape=[pltpu.VMEM(shape, f32) for shape in shapes]
        + [jax.ShapeDtypeStruct(shape, dtype) for shape, dtype in norms],
        in_specs=[pl.BlockSpec(memory_space=pltpu.VMEM)] * (len(packs) + 2),
        out_specs=[pl.BlockSpec(memory_space=pltpu.VMEM)] * len(shapes)
        + [pl.BlockSpec(shape, lambda: (0, 0)) for shape, _ in norms],
        scratch_shapes=[pltpu.VMEM(norms[2][0], f32)],
        cost_estimate=pl.CostEstimate(flops=200000000, bytes_accessed=8000000, transcendentals=0),
        name="side",
    )(*[in_vmem(x) for x in packs + norm_state])


def tail_kernel(
    t_ref, kg_ref, ke_ref, rg_ref, re_ref, lk_ref, lt_ref, lr_ref, dk_ref, dr_ref, km_ref, kw_ref, rm_ref, rw_ref,
    kc_ref, rc_ref, kv_ref, kn_ref, kp_ref, rv_ref, rn_ref, rp_ref,
):
    groups, lane_groups, _, block = t_ref.shape
    rank_size = groups * 4
    half = groups // 2
    router_rows, col_width = rm_ref.shape
    shard = lax.axis_index("shard")
    step = pl.program_id(0)
    own_lines = pl.ds(pl.multiple_of(shard * router_rows, router_rows), router_rows)

    def sums(first, lane_group):
        return jnp.concatenate([t_ref[first + i, lane_group].astype(f32) for i in range(half)], axis=0)

    def apply(left, right):
        high = left.astype(bf16)
        low = (left - high.astype(f32)).astype(bf16)
        terms = [
            lax.dot_general(term, right, (((1,), (0,)), ((), ())), preferred_element_type=f32)
            for term in (high, low)
        ]
        return terms[0] + terms[1]

    for part in range(TAIL_PARTS):
        group = step * TAIL_PARTS + part
        cols = pl.ds(pl.multiple_of(group * block, LANES), block)
        here = slice(part * block, (part + 1) * block)
        left = apply(lk_ref[...], sums(0, group).astype(bf16))
        kc_ref[0, :, here] = kg_ref[0, :, cols].astype(f32) + ke_ref[0, :, cols] - left
        left = apply(lr_ref[own_lines, :], sums(half, group).astype(bf16))
        rc_ref[0, :, here] = rg_ref[0, :, cols].astype(f32) + re_ref[0, :, cols] - left

    @pl.when(step == 0)
    def _():
        place = (lax.axis_index("z") * lax.axis_size("y") + lax.axis_index("y")) * lax.axis_size("c")
        column = (place + lax.axis_index("c")) * col_width
        lane_group = column // block
        offset = column - lane_group * block
        lines = lax.broadcasted_iota(jnp.int32, (block, LANES), 0)
        picks = lines == lax.broadcasted_iota(jnp.int32, (block, LANES), 1) + offset
        picks = picks.astype(f32).astype(bf16)

        def few(first):
            return lax.dot_general(
                sums(first, lane_group).astype(bf16), picks, (((1,), (0,)), ((), ())), preferred_element_type=f32
            )

        few_key, few_router = few(0), few(half)
        approx = dot(few_key, lt_ref[...], 0, 0)[:col_width]
        kp_ref[...] = (dk_ref[...] - learning_rate * approx).astype(bf16)
        own_lanes = pl.ds(pl.multiple_of(shard * LANES, LANES), LANES)
        own = dot(few_key, lt_ref[:, own_lanes], 0, 0)[:col_width]
        velocity = momentum_decay * km_ref[...] + own
        kv_ref[...] = velocity
        kn_ref[...] = kw_ref[...] - learning_rate * velocity
        approx = dr_ref[...] - learning_rate * dot(lr_ref[...], few_router, 1, 0)
        rp_ref[...] = approx.T[:col_width].astype(bf16)
        own = dot(lr_ref[own_lines, :], few_router, 1, 0)[:, :col_width]
        velocity = momentum_decay * rm_ref[...] + own
        rv_ref[...] = velocity
        rn_ref[...] = rw_ref[...] - learning_rate * velocity


def tail(sums, key_grad, key_error, router_grad, router_error, *small):
    lane_groups, block = sums.shape[1], sums.shape[3]
    key_rows, router_rows = key_grad.shape[1], router_grad.shape[1]
    dk, dr, km, rm = small[3], small[4], small[5], small[7]
    wide = [
        pl.BlockSpec((1, key_rows, TAIL_PARTS * block), lambda i: (0, 0, i)),
        pl.BlockSpec((1, router_rows, TAIL_PARTS * block), lambda i: (0, 0, i)),
    ]

    def whole(shape):
        return pl.BlockSpec(shape, lambda i: (0,) * len(shape))

    outs = [
        (key_grad.shape, f32),
        (router_grad.shape, f32),
        (km.shape, f32),
        (km.shape, f32),
        (dk.shape, bf16),
        (rm.shape, f32),
        (rm.shape, f32),
        ((dk.shape[0], dr.shape[0]), bf16),
    ]
    return pl.pallas_call(
        tail_kernel,
        grid=(lane_groups // TAIL_PARTS,),
        in_specs=[pl.BlockSpec(memory_space=pltpu.VMEM)] * (5 + len(small)),
        out_specs=wide + [whole(shape) for shape, _ in outs[2:]],
        out_shape=[jax.ShapeDtypeStruct(shape, dtype) for shape, dtype in outs],
        name="tail",
    )(*[in_vmem(x) for x in (sums, key_grad, key_error, router_grad, router_error) + small])


def to_all(block, axes, size):
    spread = jnp.broadcast_to(block[None], (size,) + block.shape)
    return lax.all_to_all(spread, axes, 0, 0, tiled=True)


def body(
    key_grad,
    key_error,
    router_grad,
    router_error,
    norm_grad,
    key_basis,
    router_basis,
    key_momentum,
    key_weight,
    router_momentum,
    router_weight,
    norm_momentum,
    norm_weight,
):
    n_z, n_y, n_c, n_x = (lax.axis_size(name) for name in DP + ("shard",))
    plane = n_y * n_c * n_x
    replicas = n_z * n_y * n_c
    rank_size, width = key_basis.shape
    key_rows, router_rows = key_grad.shape[1], router_grad.shape[1]
    norm_vecs, norm_width = norm_grad.shape[1:]
    col_width = key_momentum.shape[1]

    norm_lines = norm_vecs * norm_width // LANES
    router_end = rank_size + router_rows
    used = router_end + norm_lines
    pack = head(key_basis, router_basis, key_grad, key_error, router_grad, router_error, norm_grad)
    pair = lax.all_gather(pack, "c", axis=0, tiled=False)
    half = PACK_ROWS // n_c
    mine = jnp.sum(lax.dynamic_slice_in_dim(pair, lax.axis_index("c") * half, half, 1), axis=0)
    mine = jnp.sum(to_all(mine.astype(bf16), "z", n_z).astype(f32), axis=0)
    spread = to_all(mine, PAIRS, n_y * n_c).reshape(n_y, n_c, half, LANES)
    own = jnp.sum(spread, axis=0).reshape(PACK_ROWS, LANES)

    groups, lane_groups = 2 * rank_size // 8, plane // (2 * rank_size // 8)
    part, sent = mid(
        (groups, lane_groups, 8, width // lane_groups),
        own,
        key_grad,
        key_error,
        router_grad,
        router_error,
        key_momentum.T,
        key_weight.T,
        router_momentum,
        router_weight,
        norm_momentum,
        norm_weight,
    )
    part = part.reshape(plane, 8, width // lane_groups)
    near = lax.ppermute(sent, "shard", [(i, i ^ 1) for i in range(n_x)])
    part = lax.all_to_all(part, PLANE, 0, 0, tiled=True)
    mine = jnp.sum(part.astype(f32), axis=0).astype(bf16)
    mine, near = lax.optimization_barrier((mine, near))
    packs = jnp.stack([sent, near])
    far = lax.ppermute(packs, "shard", [(i, i ^ 2) for i in range(n_x)])
    *lefts, norm_velocity, norm_master, norm_params = side(
        [packs, far], [norm_momentum, norm_weight], replicas, rank_size, router_rows, col_width
    )
    mine = jnp.sum(to_all(mine, "z", n_z).astype(f32), axis=0).astype(bf16)
    mine, lefts, norm_velocity, norm_master, norm_params = lax.optimization_barrier(
        (mine, lefts, norm_velocity, norm_master, norm_params)
    )
    sums = to_all(mine, PLANE, plane).reshape(groups, lane_groups, 8, width // lane_groups)
    (key_carry, router_carry, key_velocity, key_master, key_params, router_velocity, router_master, router_params) = (
        tail(
            sums,
            key_grad,
            key_error,
            router_grad,
            router_error,
            *lefts,
            key_momentum.T,
            key_weight.T,
            router_momentum,
            router_weight,
        )
    )

    return (
        key_carry,
        router_carry,
        key_velocity.T,
        key_master.T,
        key_params.T,
        router_velocity,
        router_master,
        router_params.T,
        norm_velocity,
        norm_master,
        norm_params,
    )


def solution(mesh):
    n_dp, n_x = mesh.devices.shape
    fine = Mesh(mesh.devices.reshape(n_dp // 8, 4, 2, n_x), DP + ("shard",))
    return jax.shard_map(
        body,
        mesh=fine,
        in_specs=(
            P(DP, "shard", None),
            P(DP, "shard", None),
            P(DP, "shard", None),
            P(DP, "shard", None),
            P(DP, None, "shard"),
            P(),
            P(),
            P("shard", DP),
            P("shard", DP),
            P("shard", DP),
            P("shard", DP),
            P(None, "shard"),
            P(None, "shard"),
        ),
        out_specs=(
            P(DP, "shard", None),
            P(DP, "shard", None),
            P("shard", DP),
            P("shard", DP),
            P(None, DP),
            P("shard", DP),
            P("shard", DP),
            P(None, DP),
            P(None, "shard"),
            P(None, "shard"),
            P(),
        ),
        check_vma=False,
    )
```

```python
import jax
import jax.numpy as jnp
from jax import lax
from jax.experimental import pallas as pl
from jax.experimental.pallas import tpu as pltpu
from jax.sharding import Mesh, PartitionSpec as P

ROOT_STEPS = 4

highest = lax.Precision.HIGHEST
momentum_decay = 0.9
learning_rate = 0.1
f32 = jnp.float32
bf16 = jnp.bfloat16

DP = ("z", "y", "c")
PAIRS = ("y", "c")
CHIPS = ("y", "shard")
PLANE = ("c",) + CHIPS
LANES = 128
TAIL_PARTS = 2
PACK_ROWS = 48
KEY_AT, ROUTER_AT, NORM_AT = 48, 72, 88


def dot(left, right, left_dim, right_dim):
    return lax.dot_general(left, right, (((left_dim,), (right_dim,)), ((), ())), precision=highest)


def in_halves(left, right, left_dim, right_dim):
    left_high, right_high = left.astype(bf16), right.astype(bf16)
    left_low = (left - left_high.astype(f32)).astype(bf16)
    right_low = (right - right_high.astype(f32)).astype(bf16)
    total = 0.0
    for one, other in ((left_low, right_high), (left_high, right_low), (left_high, right_high)):
        total = total + lax.dot_general(
            one, other, (((left_dim,), (right_dim,)), ((), ())), preferred_element_type=f32
        )
    return total


def in_vmem(array):
    return pltpu.with_memory_space_constraint(array, pltpu.VMEM)


def head_kernel(kb_ref, rb_ref, kg_ref, ke_ref, rg_ref, re_ref, ng_ref, out_ref):
    rank_size, router_rows = kb_ref.shape[0], rg_ref.shape[1]
    norm_vecs, norm_width = ng_ref.shape[1:]
    router_end = rank_size + router_rows

    @pl.when(pl.program_id(0) == 0)
    def _():
        out_ref[...] = jnp.zeros_like(out_ref)
        norm = jnp.concatenate([ng_ref[0].astype(f32), jnp.zeros((8 - norm_vecs, norm_width), f32)], axis=0)
        pieces = router_rows // norm_vecs
        piece = norm_width // pieces
        lane = lax.broadcasted_iota(jnp.int32, (8, LANES), 1)
        for index in range(pieces):
            line = pltpu.roll(norm, (rank_size - index * piece) % norm_width, 1)[:, :LANES]
            line = jnp.where((lane >= rank_size) & (lane < rank_size + piece), line, 0.0)
            for vec in range(norm_vecs):
                row = rank_size + vec * pieces + index
                out_ref[row : row + 1, :] = line[vec : vec + 1]

    merged_key = kg_ref[0].astype(f32) + ke_ref[0]
    merged_router = rg_ref[0].astype(f32) + re_ref[0]
    out_ref[:rank_size, :] += in_halves(kb_ref[...], merged_key, 1, 1)
    out_ref[rank_size:router_end, :rank_size] += in_halves(merged_router, rb_ref[...], 1, 1)


def head(key_basis, router_basis, key_grad, key_error, router_grad, router_error, norm_grad):
    rank_size, width = key_basis.shape
    key_rows, router_rows = key_grad.shape[1], router_grad.shape[1]
    steps = 2
    block = width // steps
    return pl.pallas_call(
        head_kernel,
        grid=(steps,),
        in_specs=[
            pl.BlockSpec((rank_size, block), lambda i: (0, i)),
            pl.BlockSpec((rank_size, block), lambda i: (0, i)),
            pl.BlockSpec((1, key_rows, block), lambda i: (0, 0, i)),
            pl.BlockSpec((1, key_rows, block), lambda i: (0, 0, i)),
            pl.BlockSpec((1, router_rows, block), lambda i: (0, 0, i)),
            pl.BlockSpec((1, router_rows, block), lambda i: (0, 0, i)),
            pl.BlockSpec(norm_grad.shape, lambda i: (0, 0, 0)),
        ],
        out_specs=pl.BlockSpec(memory_space=pltpu.VMEM),
        out_shape=pltpu.VMEM((PACK_ROWS, LANES), f32),
        name="head",
    )(key_basis, router_basis, key_grad, key_error, router_grad, router_error, norm_grad)


def mid_kernel(
    own_ref, kg_ref, ke_ref, rg_ref, re_ref, km_ref, kw_ref, rm_ref, rw_ref, nm_ref, nw_ref, part_ref, sent_ref
):
    groups, lane_groups, lines, block = part_ref.shape
    half, (router_rows, col_width) = groups // 2, rm_ref.shape
    rank_size = half * lines
    key_rows = own_ref[:rank_size, :]
    rout_rows = own_ref[rank_size : rank_size + router_rows, :rank_size]
    for group in range(lane_groups):
        cols = slice(group * block, (group + 1) * block)
        key_part = in_halves(key_rows, kg_ref[0, :, cols].astype(f32) + ke_ref[0, :, cols], 1, 0)
        rout_part = in_halves(rout_rows, rg_ref[0, :, cols].astype(f32) + re_ref[0, :, cols], 0, 0)
        for i in range(half):
            part_ref[i, group] = key_part[i * lines : (i + 1) * lines].astype(bf16)
            part_ref[half + i, group] = rout_part[i * lines : (i + 1) * lines].astype(bf16)
    decay = learning_rate * momentum_decay
    sent_ref[:KEY_AT, :] = own_ref[...]
    sent_ref[KEY_AT:, :] = jnp.zeros((sent_ref.shape[0] - KEY_AT, LANES), f32)
    sent_ref[KEY_AT : KEY_AT + col_width, :] = kw_ref[...] - decay * km_ref[...]
    sent_ref[ROUTER_AT : ROUTER_AT + router_rows, :col_width] = rw_ref[...] - decay * rm_ref[...]
    norm = nw_ref[...] - decay * nm_ref[...]
    norm_vecs, norm_width = norm.shape
    for vec in range(norm_vecs):
        for first in range(0, norm_width, LANES):
            row = NORM_AT + (vec * norm_width + first) // LANES
            sent_ref[row : row + 1, :] = norm[vec : vec + 1, first : first + LANES]


def mid(chunks, *operands):
    return pl.pallas_call(
        mid_kernel,
        in_specs=[pl.BlockSpec(memory_space=pltpu.VMEM)] * len(operands),
        out_specs=[pl.BlockSpec(chunks, lambda: (0,) * len(chunks)), pl.BlockSpec(memory_space=pltpu.VMEM)],
        out_shape=[jax.ShapeDtypeStruct(chunks, bf16), pltpu.VMEM((NORM_AT + 16, LANES), f32)],
        name="mid",
    )(*[in_vmem(x) for x in operands])


def square_of_root(gram, replicas):
    scaling = jnp.sqrt(jnp.sum(gram * gram, axis=(0, 1), keepdims=True)) + 1e-06
    rows = lax.broadcasted_iota(jnp.int32, gram.shape, 0)
    identity = (rows == lax.broadcasted_iota(jnp.int32, gram.shape, 1)).astype(f32)
    square_side, root_side = gram / scaling, identity
    for sweep_index in range(ROOT_STEPS):
        middle = 1.5 * identity - 0.5 * dot(root_side, square_side, 1, 0)
        square_side = dot(square_side, middle, 1, 0)
        root_side = dot(middle, root_side, 1, 0)
    return dot(root_side, root_side, 0, 0) / (scaling * replicas)


def norm_rows(lines, start, norm_vecs, norm_width):
    pieces = lines.shape[0] // norm_vecs
    piece = norm_width // pieces
    lane = lax.broadcasted_iota(jnp.int32, lines.shape, 1)
    lines = jnp.where((lane >= start) & (lane < start + piece), lines, 0.0)
    lines = jnp.concatenate([lines, jnp.zeros((lines.shape[0], norm_width - LANES), f32)], axis=1)
    totals = [0.0] * norm_vecs
    for index in range(pieces):
        moved = pltpu.roll(lines, (index * piece - start) % norm_width, 1)
        for vec in range(norm_vecs):
            row = vec * pieces + index
            totals[vec] = totals[vec] + moved[row : row + 1]
    return totals


def side_kernel(replicas, rank_size, router_rows, col_width, *refs):
    packs = [ref.at[i] for ref in refs[:2] for i in range(2)]
    nm_ref, nw_ref, lk_ref, lt_ref, lr_ref, dk_ref, dr_ref, nv_ref, nn_ref, np_ref, wide_ref = refs[2:]
    norm_vecs, norm_width = nm_ref.shape
    router_end = rank_size + router_rows
    shard = lax.axis_index("shard")
    key_rows = [pack[:rank_size, :] for pack in packs]
    rout_rows = [pack[rank_size:router_end, :rank_size] for pack in packs]
    square_key = square_of_root(sum(dot(rows, rows, 1, 1) for rows in key_rows), replicas)
    square_router = square_of_root(sum(dot(rows, rows, 0, 0) for rows in rout_rows), replicas)
    lk_ref[...] = dot(key_rows[0], square_key, 0, 0)
    for distance, pack in enumerate(packs):
        place = lax.bitwise_xor(shard, distance)
        lanes = pl.ds(pl.multiple_of(place * LANES, LANES), LANES)
        lines = pl.ds(pl.multiple_of(place * router_rows, router_rows), router_rows)
        lt_ref[:, lanes] = dot(square_key, key_rows[distance], 0, 0)
        lr_ref[lines, :] = dot(rout_rows[distance], square_router, 1, 0)
        dk_ref[:, lanes] = pack[KEY_AT : KEY_AT + col_width, :]
        dr_ref[lines, :] = pack[ROUTER_AT : ROUTER_AT + router_rows, :]
        means = norm_rows(pack[rank_size:router_end, :], rank_size, norm_vecs, norm_width)
        for vec, mean in enumerate(means):
            mean = mean / replicas
            for first in range(0, norm_width, LANES):
                here = slice(first, first + LANES)
                row = NORM_AT + (vec * norm_width + first) // LANES
                lanes = pl.ds(pl.multiple_of(place * norm_width + first, LANES), LANES)
                wide_ref[vec : vec + 1, lanes] = pack[row : row + 1, :] - learning_rate * mean[:, here]
            if distance == 0:
                velocity = momentum_decay * nm_ref[vec : vec + 1, :] + mean
                nv_ref[vec : vec + 1, :] = velocity
                nn_ref[vec : vec + 1, :] = nw_ref[vec : vec + 1, :] - learning_rate * velocity
    np_ref[...] = wide_ref[...].astype(bf16)


def side(packs, norm_state, replicas, rank_size, router_rows, col_width):
    n_x = 2 * len(packs)
    shapes = [
        (LANES, rank_size),
        (rank_size, n_x * LANES),
        (n_x * router_rows, rank_size),
        (col_width, n_x * LANES),
        (n_x * router_rows, LANES),
    ]
    norm_vecs, norm_width = norm_state[0].shape
    norms = [((norm_vecs, norm_width), f32)] * 2 + [((norm_vecs, n_x * norm_width), bf16)]
    return pl.pallas_call(
        lambda *refs: side_kernel(replicas, rank_size, router_rows, col_width, *refs),
        out_shape=[pltpu.VMEM(shape, f32) for shape in shapes]
        + [jax.ShapeDtypeStruct(shape, dtype) for shape, dtype in norms],
        in_specs=[pl.BlockSpec(memory_space=pltpu.VMEM)] * (len(packs) + 2),
        out_specs=[pl.BlockSpec(memory_space=pltpu.VMEM)] * len(shapes)
        + [pl.BlockSpec(shape, lambda: (0, 0)) for shape, _ in norms],
        scratch_shapes=[pltpu.VMEM(norms[2][0], f32)],
        cost_estimate=pl.CostEstimate(flops=200000000, bytes_accessed=8000000, transcendentals=0),
        name="side",
    )(*[in_vmem(x) for x in packs + norm_state])


def tail_kernel(
    t_ref, kg_ref, ke_ref, rg_ref, re_ref, lk_ref, lt_ref, lr_ref, dk_ref, dr_ref, km_ref, kw_ref, rm_ref, rw_ref,
    kc_ref, rc_ref, kv_ref, kn_ref, kp_ref, rv_ref, rn_ref, rp_ref,
):
    groups, lane_groups, _, block = t_ref.shape
    rank_size = groups * 4
    half = groups // 2
    router_rows, col_width = rm_ref.shape
    shard = lax.axis_index("shard")
    step = pl.program_id(0)
    own_lines = pl.ds(pl.multiple_of(shard * router_rows, router_rows), router_rows)

    def sums(first, lane_group):
        return jnp.concatenate([t_ref[first + i, lane_group].astype(f32) for i in range(half)], axis=0)

    def apply(left, right):
        high = left.astype(bf16)
        low = (left - high.astype(f32)).astype(bf16)
        terms = [
            lax.dot_general(term, right, (((1,), (0,)), ((), ())), preferred_element_type=f32)
            for term in (high, low)
        ]
        return terms[0] + terms[1]

    for part in range(TAIL_PARTS):
        group = step * TAIL_PARTS + part
        cols = pl.ds(pl.multiple_of(group * block, LANES), block)
        here = slice(part * block, (part + 1) * block)
        left = apply(lk_ref[...], sums(0, group).astype(bf16))
        kc_ref[0, :, here] = kg_ref[0, :, cols].astype(f32) + ke_ref[0, :, cols] - left
        left = apply(lr_ref[own_lines, :], sums(half, group).astype(bf16))
        rc_ref[0, :, here] = rg_ref[0, :, cols].astype(f32) + re_ref[0, :, cols] - left

    @pl.when(step == 0)
    def _():
        place = (lax.axis_index("z") * lax.axis_size("y") + lax.axis_index("y")) * lax.axis_size("c")
        column = (place + lax.axis_index("c")) * col_width
        lane_group = column // block
        offset = column - lane_group * block
        lines = lax.broadcasted_iota(jnp.int32, (block, LANES), 0)
        picks = lines == lax.broadcasted_iota(jnp.int32, (block, LANES), 1) + offset
        picks = picks.astype(f32).astype(bf16)

        def few(first):
            return lax.dot_general(
                sums(first, lane_group).astype(bf16), picks, (((1,), (0,)), ((), ())), preferred_element_type=f32
            )

        few_key, few_router = few(0), few(half)
        approx = dot(few_key, lt_ref[...], 0, 0)[:col_width]
        kp_ref[...] = (dk_ref[...] - learning_rate * approx).astype(bf16)
        own_lanes = pl.ds(pl.multiple_of(shard * LANES, LANES), LANES)
        own = dot(few_key, lt_ref[:, own_lanes], 0, 0)[:col_width]
        velocity = momentum_decay * km_ref[...] + own
        kv_ref[...] = velocity
        kn_ref[...] = kw_ref[...] - learning_rate * velocity
        approx = dr_ref[...] - learning_rate * dot(lr_ref[...], few_router, 1, 0)
        rp_ref[...] = approx.T[:col_width].astype(bf16)
        own = dot(lr_ref[own_lines, :], few_router, 1, 0)[:, :col_width]
        velocity = momentum_decay * rm_ref[...] + own
        rv_ref[...] = velocity
        rn_ref[...] = rw_ref[...] - learning_rate * velocity


def tail(sums, key_grad, key_error, router_grad, router_error, *small):
    lane_groups, block = sums.shape[1], sums.shape[3]
    key_rows, router_rows = key_grad.shape[1], router_grad.shape[1]
    dk, dr, km, rm = small[3], small[4], small[5], small[7]
    wide = [
        pl.BlockSpec((1, key_rows, TAIL_PARTS * block), lambda i: (0, 0, i)),
        pl.BlockSpec((1, router_rows, TAIL_PARTS * block), lambda i: (0, 0, i)),
    ]

    def whole(shape):
        return pl.BlockSpec(shape, lambda i: (0,) * len(shape))

    outs = [
        (key_grad.shape, f32),
        (router_grad.shape, f32),
        (km.shape, f32),
        (km.shape, f32),
        (dk.shape, bf16),
        (rm.shape, f32),
        (rm.shape, f32),
        ((dk.shape[0], dr.shape[0]), bf16),
    ]
    return pl.pallas_call(
        tail_kernel,
        grid=(lane_groups // TAIL_PARTS,),
        in_specs=[pl.BlockSpec(memory_space=pltpu.VMEM)] * (5 + len(small)),
        out_specs=wide + [whole(shape) for shape, _ in outs[2:]],
        out_shape=[jax.ShapeDtypeStruct(shape, dtype) for shape, dtype in outs],
        name="tail",
    )(*[in_vmem(x) for x in (sums, key_grad, key_error, router_grad, router_error) + small])


def to_all(block, axes, size):
    spread = jnp.broadcast_to(block[None], (size,) + block.shape)
    return lax.all_to_all(spread, axes, 0, 0, tiled=True)


def body(
    key_grad,
    key_error,
    router_grad,
    router_error,
    norm_grad,
    key_basis,
    router_basis,
    key_momentum,
    key_weight,
    router_momentum,
    router_weight,
    norm_momentum,
    norm_weight,
):
    n_z, n_y, n_c, n_x = (lax.axis_size(name) for name in DP + ("shard",))
    plane = n_y * n_c * n_x
    replicas = n_z * n_y * n_c
    rank_size, width = key_basis.shape
    key_rows, router_rows = key_grad.shape[1], router_grad.shape[1]
    norm_vecs, norm_width = norm_grad.shape[1:]
    col_width = key_momentum.shape[1]

    router_end = rank_size + router_rows
    pack = head(key_basis, router_basis, key_grad, key_error, router_grad, router_error, norm_grad)
    pair = lax.all_gather(pack, "c", axis=0, tiled=False)
    half = PACK_ROWS // n_c
    mine = jnp.sum(lax.dynamic_slice_in_dim(pair, lax.axis_index("c") * half, half, 1), axis=0)
    mine = jnp.sum(to_all(mine.astype(bf16), "z", n_z).astype(f32), axis=0)
    spread = to_all(mine, PAIRS, n_y * n_c).reshape(n_y, n_c, half, LANES)
    own = jnp.sum(spread, axis=0).reshape(PACK_ROWS, LANES)

    groups, lane_groups = 2 * rank_size // 8, plane // (2 * rank_size // 8)
    part, sent = mid(
        (groups, lane_groups, 8, width // lane_groups),
        own,
        key_grad,
        key_error,
        router_grad,
        router_error,
        key_momentum.T,
        key_weight.T,
        router_momentum,
        router_weight,
        norm_momentum,
        norm_weight,
    )
    part = part.reshape(plane, 8, width // lane_groups)
    near = lax.ppermute(sent, "shard", [(i, i ^ 1) for i in range(n_x)])
    part = lax.all_to_all(part, PLANE, 0, 0, tiled=True)
    mine = jnp.sum(part.astype(f32), axis=0).astype(bf16)
    mine, near = lax.optimization_barrier((mine, near))
    packs = jnp.stack([sent, near])
    far = lax.ppermute(packs, "shard", [(i, i ^ 2) for i in range(n_x)])
    *lefts, norm_velocity, norm_master, norm_params = side(
        [packs, far], [norm_momentum, norm_weight], replicas, rank_size, router_rows, col_width
    )
    mine = jnp.sum(to_all(mine, "z", n_z).astype(f32), axis=0).astype(bf16)
    mine, lefts, norm_velocity, norm_master, norm_params = lax.optimization_barrier(
        (mine, lefts, norm_velocity, norm_master, norm_params)
    )
    sums = lax.all_gather(to_all(mine, CHIPS, n_y * n_x), "c", axis=0, tiled=False)
    sums = sums.reshape(groups, lane_groups, 8, width // lane_groups)
    (key_carry, router_carry, key_velocity, key_master, key_params, router_velocity, router_master, router_params) = (
        tail(
            sums,
            key_grad,
            key_error,
            router_grad,
            router_error,
            *lefts,
            key_momentum.T,
            key_weight.T,
            router_momentum,
            router_weight,
        )
    )

    return (
        key_carry,
        router_carry,
        key_velocity.T,
        key_master.T,
        key_params.T,
        router_velocity,
        router_master,
        router_params.T,
        norm_velocity,
        norm_master,
        norm_params,
    )


def solution(mesh):
    n_dp, n_x = mesh.devices.shape
    fine = Mesh(mesh.devices.reshape(n_dp // 8, 4, 2, n_x), DP + ("shard",))
    return jax.shard_map(
        body,
        mesh=fine,
        in_specs=(
            P(DP, "shard", None),
            P(DP, "shard", None),
            P(DP, "shard", None),
            P(DP, "shard", None),
            P(DP, None, "shard"),
            P(),
            P(),
            P("shard", DP),
            P("shard", DP),
            P("shard", DP),
            P("shard", DP),
            P(None, "shard"),
            P(None, "shard"),
        ),
        out_specs=(
            P(DP, "shard", None),
            P(DP, "shard", None),
            P("shard", DP),
            P("shard", DP),
            P(None, DP),
            P("shard", DP),
            P("shard", DP),
            P(None, DP),
            P(None, "shard"),
            P(None, "shard"),
            P(),
        ),
        check_vma=False,
    )
```

```python
import jax
import jax.numpy as jnp
from jax import lax
from jax.experimental import pallas as pl
from jax.experimental.pallas import tpu as pltpu
from jax.sharding import Mesh, PartitionSpec as P

ROOT_STEPS = 4

highest = lax.Precision.HIGHEST
momentum_decay = 0.9
learning_rate = 0.1
f32 = jnp.float32
bf16 = jnp.bfloat16

DP = ("z", "y", "c")
PAIRS = ("y", "c")
CHIPS = ("y", "shard")
PLANE = ("c",) + CHIPS
LANES = 128
TAIL_PARTS = 2
PACK_ROWS = 48
KEY_AT, ROUTER_AT, NORM_AT = 48, 72, 88


def dot(left, right, left_dim, right_dim):
    return lax.dot_general(left, right, (((left_dim,), (right_dim,)), ((), ())), precision=highest)


def in_halves(left, right, left_dim, right_dim):
    left_high, right_high = left.astype(bf16), right.astype(bf16)
    left_low = (left - left_high.astype(f32)).astype(bf16)
    right_low = (right - right_high.astype(f32)).astype(bf16)
    total = 0.0
    for one, other in ((left_low, right_high), (left_high, right_low), (left_high, right_high)):
        total = total + lax.dot_general(
            one, other, (((left_dim,), (right_dim,)), ((), ())), preferred_element_type=f32
        )
    return total


def in_vmem(array):
    return pltpu.with_memory_space_constraint(array, pltpu.VMEM)


def head_kernel(kb_ref, rb_ref, kg_ref, ke_ref, rg_ref, re_ref, ng_ref, out_ref):
    rank_size, router_rows = kb_ref.shape[0], rg_ref.shape[1]
    norm_vecs, norm_width = ng_ref.shape[1:]
    router_end = rank_size + router_rows

    @pl.when(pl.program_id(0) == 0)
    def _():
        out_ref[...] = jnp.zeros_like(out_ref)
        norm = jnp.concatenate([ng_ref[0].astype(f32), jnp.zeros((8 - norm_vecs, norm_width), f32)], axis=0)
        pieces = router_rows // norm_vecs
        piece = norm_width // pieces
        lane = lax.broadcasted_iota(jnp.int32, (8, LANES), 1)
        for index in range(pieces):
            line = pltpu.roll(norm, (rank_size - index * piece) % norm_width, 1)[:, :LANES]
            line = jnp.where((lane >= rank_size) & (lane < rank_size + piece), line, 0.0)
            for vec in range(norm_vecs):
                row = rank_size + vec * pieces + index
                out_ref[row : row + 1, :] = line[vec : vec + 1]

    merged_key = kg_ref[0].astype(f32) + ke_ref[0]
    merged_router = rg_ref[0].astype(f32) + re_ref[0]
    out_ref[:rank_size, :] += in_halves(kb_ref[...], merged_key, 1, 1)
    out_ref[rank_size:router_end, :rank_size] += in_halves(merged_router, rb_ref[...], 1, 1)


def head(key_basis, router_basis, key_grad, key_error, router_grad, router_error, norm_grad):
    rank_size, width = key_basis.shape
    key_rows, router_rows = key_grad.shape[1], router_grad.shape[1]
    steps = 2
    block = width // steps
    return pl.pallas_call(
        head_kernel,
        grid=(steps,),
        in_specs=[
            pl.BlockSpec((rank_size, block), lambda i: (0, i)),
            pl.BlockSpec((rank_size, block), lambda i: (0, i)),
            pl.BlockSpec((1, key_rows, block), lambda i: (0, 0, i)),
            pl.BlockSpec((1, key_rows, block), lambda i: (0, 0, i)),
            pl.BlockSpec((1, router_rows, block), lambda i: (0, 0, i)),
            pl.BlockSpec((1, router_rows, block), lambda i: (0, 0, i)),
            pl.BlockSpec(norm_grad.shape, lambda i: (0, 0, 0)),
        ],
        out_specs=pl.BlockSpec(memory_space=pltpu.VMEM),
        out_shape=pltpu.VMEM((PACK_ROWS, LANES), f32),
        name="head",
    )(key_basis, router_basis, key_grad, key_error, router_grad, router_error, norm_grad)


def mid_kernel(
    own_ref, kg_ref, ke_ref, rg_ref, re_ref, km_ref, kw_ref, rm_ref, rw_ref, nm_ref, nw_ref, part_ref, sent_ref
):
    groups, lane_groups, lines, block = part_ref.shape
    half, (router_rows, col_width) = groups // 2, rm_ref.shape
    rank_size = half * lines
    key_rows = own_ref[:rank_size, :]
    rout_rows = own_ref[rank_size : rank_size + router_rows, :rank_size]
    for group in range(lane_groups):
        cols = slice(group * block, (group + 1) * block)
        key_part = in_halves(key_rows, kg_ref[0, :, cols].astype(f32) + ke_ref[0, :, cols], 1, 0)
        rout_part = in_halves(rout_rows, rg_ref[0, :, cols].astype(f32) + re_ref[0, :, cols], 0, 0)
        for i in range(half):
            part_ref[i, group] = key_part[i * lines : (i + 1) * lines].astype(bf16)
            part_ref[half + i, group] = rout_part[i * lines : (i + 1) * lines].astype(bf16)
    decay = learning_rate * momentum_decay
    sent_ref[:KEY_AT, :] = own_ref[...]
    sent_ref[KEY_AT:, :] = jnp.zeros((sent_ref.shape[0] - KEY_AT, LANES), f32)
    sent_ref[KEY_AT : KEY_AT + col_width, :] = kw_ref[...] - decay * km_ref[...]
    sent_ref[ROUTER_AT : ROUTER_AT + router_rows, :col_width] = rw_ref[...] - decay * rm_ref[...]
    norm = nw_ref[...] - decay * nm_ref[...]
    norm_vecs, norm_width = norm.shape
    for vec in range(norm_vecs):
        for first in range(0, norm_width, LANES):
            row = NORM_AT + (vec * norm_width + first) // LANES
            sent_ref[row : row + 1, :] = norm[vec : vec + 1, first : first + LANES]


def mid(chunks, *operands):
    return pl.pallas_call(
        mid_kernel,
        in_specs=[pl.BlockSpec(memory_space=pltpu.VMEM)] * len(operands),
        out_specs=[pl.BlockSpec(memory_space=pltpu.VMEM)] * 2,
        out_shape=[pltpu.VMEM(chunks, bf16), pltpu.VMEM((NORM_AT + 16, LANES), f32)],
        name="mid",
    )(*[in_vmem(x) for x in operands])


def square_of_root(gram, replicas):
    scaling = jnp.sqrt(jnp.sum(gram * gram, axis=(0, 1), keepdims=True)) + 1e-06
    rows = lax.broadcasted_iota(jnp.int32, gram.shape, 0)
    identity = (rows == lax.broadcasted_iota(jnp.int32, gram.shape, 1)).astype(f32)
    square_side, root_side = gram / scaling, identity
    for sweep_index in range(ROOT_STEPS):
        if sweep_index == 0:
            middle = 1.5 * identity - 0.5 * square_side
            root_side = middle
        else:
            middle = 1.5 * identity - 0.5 * dot(root_side, square_side, 1, 0)
            root_side = dot(middle, root_side, 1, 0)
        if sweep_index < ROOT_STEPS - 1:
            square_side = dot(square_side, middle, 1, 0)
    return dot(root_side, root_side, 0, 0) / (scaling * replicas)


def norm_rows(lines, start, norm_vecs, norm_width):
    pieces = lines.shape[0] // norm_vecs
    piece = norm_width // pieces
    lane = lax.broadcasted_iota(jnp.int32, lines.shape, 1)
    lines = jnp.where((lane >= start) & (lane < start + piece), lines, 0.0)
    lines = jnp.concatenate([lines, jnp.zeros((lines.shape[0], norm_width - LANES), f32)], axis=1)
    totals = [0.0] * norm_vecs
    for index in range(pieces):
        moved = pltpu.roll(lines, (index * piece - start) % norm_width, 1)
        for vec in range(norm_vecs):
            row = vec * pieces + index
            totals[vec] = totals[vec] + moved[row : row + 1]
    return totals


def side_kernel(replicas, rank_size, router_rows, col_width, *refs):
    packs = [ref.at[i] for ref in refs[:2] for i in range(2)]
    nm_ref, nw_ref, lk_ref, lt_ref, lr_ref, dk_ref, dr_ref, nv_ref, nn_ref, np_ref, wide_ref = refs[2:]
    norm_vecs, norm_width = nm_ref.shape
    router_end = rank_size + router_rows
    shard = lax.axis_index("shard")
    key_rows = [pack[:rank_size, :] for pack in packs]
    rout_rows = [pack[rank_size:router_end, :rank_size] for pack in packs]
    square_key = square_of_root(sum(dot(rows, rows, 1, 1) for rows in key_rows), replicas)
    square_router = square_of_root(sum(dot(rows, rows, 0, 0) for rows in rout_rows), replicas)
    lk_ref[...] = dot(key_rows[0], square_key, 0, 0)
    for distance, pack in enumerate(packs):
        place = lax.bitwise_xor(shard, distance)
        lanes = pl.ds(pl.multiple_of(place * LANES, LANES), LANES)
        lines = pl.ds(pl.multiple_of(place * router_rows, router_rows), router_rows)
        lt_ref[:, lanes] = dot(square_key, key_rows[distance], 0, 0)
        lr_ref[lines, :] = dot(rout_rows[distance], square_router, 1, 0)
        dk_ref[:, lanes] = pack[KEY_AT : KEY_AT + col_width, :]
        dr_ref[lines, :] = pack[ROUTER_AT : ROUTER_AT + router_rows, :]
        means = norm_rows(pack[rank_size:router_end, :], rank_size, norm_vecs, norm_width)
        for vec, mean in enumerate(means):
            mean = mean / replicas
            for first in range(0, norm_width, LANES):
                here = slice(first, first + LANES)
                row = NORM_AT + (vec * norm_width + first) // LANES
                lanes = pl.ds(pl.multiple_of(place * norm_width + first, LANES), LANES)
                wide_ref[vec : vec + 1, lanes] = pack[row : row + 1, :] - learning_rate * mean[:, here]
            if distance == 0:
                velocity = momentum_decay * nm_ref[vec : vec + 1, :] + mean
                nv_ref[vec : vec + 1, :] = velocity
                nn_ref[vec : vec + 1, :] = nw_ref[vec : vec + 1, :] - learning_rate * velocity
    np_ref[...] = wide_ref[...].astype(bf16)


def side(packs, norm_state, replicas, rank_size, router_rows, col_width):
    n_x = 2 * len(packs)
    shapes = [
        (LANES, rank_size),
        (rank_size, n_x * LANES),
        (n_x * router_rows, rank_size),
        (col_width, n_x * LANES),
        (n_x * router_rows, LANES),
    ]
    norm_vecs, norm_width = norm_state[0].shape
    norms = [((norm_vecs, norm_width), f32)] * 2 + [((norm_vecs, n_x * norm_width), bf16)]
    return pl.pallas_call(
        lambda *refs: side_kernel(replicas, rank_size, router_rows, col_width, *refs),
        out_shape=[pltpu.VMEM(shape, f32) for shape in shapes]
        + [jax.ShapeDtypeStruct(shape, dtype) for shape, dtype in norms],
        in_specs=[pl.BlockSpec(memory_space=pltpu.VMEM)] * (len(packs) + 2),
        out_specs=[pl.BlockSpec(memory_space=pltpu.VMEM)] * len(shapes)
        + [pl.BlockSpec(shape, lambda: (0, 0)) for shape, _ in norms],
        scratch_shapes=[pltpu.VMEM(norms[2][0], f32)],
        cost_estimate=pl.CostEstimate(flops=200000000, bytes_accessed=8000000, transcendentals=0),
        name="side",
    )(*[in_vmem(x) for x in packs + norm_state])


def spread_kernel(part_ref, out_ref):
    total = jnp.sum(part_ref[...].astype(f32), axis=0).astype(bf16)
    for place in range(out_ref.shape[0]):
        out_ref[place] = total


def spread_sum(part, size):
    return pl.pallas_call(
        spread_kernel,
        in_specs=[pl.BlockSpec(memory_space=pltpu.VMEM)],
        out_specs=pl.BlockSpec(memory_space=pltpu.VMEM),
        out_shape=pltpu.VMEM((size,) + part.shape[1:], bf16),
        name="spread",
    )(in_vmem(part))


def tail_kernel(
    t_ref, kg_ref, ke_ref, rg_ref, re_ref, lk_ref, lt_ref, lr_ref, dk_ref, dr_ref, km_ref, kw_ref, rm_ref, rw_ref,
    kc_ref, rc_ref, kv_ref, kn_ref, kp_ref, rv_ref, rn_ref, rp_ref,
):
    groups, lane_groups, _, block = t_ref.shape
    rank_size = groups * 4
    half = groups // 2
    router_rows, col_width = rm_ref.shape
    shard = lax.axis_index("shard")
    step = pl.program_id(0)
    own_lines = pl.ds(pl.multiple_of(shard * router_rows, router_rows), router_rows)

    def sums(first, lane_group):
        return jnp.concatenate([t_ref[first + i, lane_group].astype(f32) for i in range(half)], axis=0)

    def apply(left, right):
        high = left.astype(bf16)
        low = (left - high.astype(f32)).astype(bf16)
        terms = [
            lax.dot_general(term, right, (((1,), (0,)), ((), ())), preferred_element_type=f32)
            for term in (high, low)
        ]
        return terms[0] + terms[1]

    for part in range(TAIL_PARTS):
        group = step * TAIL_PARTS + part
        cols = pl.ds(pl.multiple_of(group * block, LANES), block)
        here = slice(part * block, (part + 1) * block)
        left = apply(lk_ref[...], sums(0, group).astype(bf16))
        kc_ref[0, :, here] = kg_ref[0, :, cols].astype(f32) + ke_ref[0, :, cols] - left
        left = apply(lr_ref[own_lines, :], sums(half, group).astype(bf16))
        rc_ref[0, :, here] = rg_ref[0, :, cols].astype(f32) + re_ref[0, :, cols] - left

    @pl.when(step == 0)
    def _():
        place = (lax.axis_index("z") * lax.axis_size("y") + lax.axis_index("y")) * lax.axis_size("c")
        column = (place + lax.axis_index("c")) * col_width
        lane_group = column // block
        offset = column - lane_group * block
        lines = lax.broadcasted_iota(jnp.int32, (block, LANES), 0)
        picks = lines == lax.broadcasted_iota(jnp.int32, (block, LANES), 1) + offset
        picks = picks.astype(f32).astype(bf16)

        def few(first):
            return lax.dot_general(
                sums(first, lane_group).astype(bf16), picks, (((1,), (0,)), ((), ())), preferred_element_type=f32
            )

        few_key, few_router = few(0), few(half)
        approx = dot(few_key, lt_ref[...], 0, 0)[:col_width]
        kp_ref[...] = (dk_ref[...] - learning_rate * approx).astype(bf16)
        own_lanes = pl.ds(pl.multiple_of(shard * LANES, LANES), LANES)
        own = dot(few_key, lt_ref[:, own_lanes], 0, 0)[:col_width]
        velocity = momentum_decay * km_ref[...] + own
        kv_ref[...] = velocity
        kn_ref[...] = kw_ref[...] - learning_rate * velocity
        approx = dr_ref[...] - learning_rate * dot(lr_ref[...], few_router, 1, 0)
        rp_ref[...] = approx.T[:col_width].astype(bf16)
        own = dot(lr_ref[own_lines, :], few_router, 1, 0)[:, :col_width]
        velocity = momentum_decay * rm_ref[...] + own
        rv_ref[...] = velocity
        rn_ref[...] = rw_ref[...] - learning_rate * velocity


def tail(sums, key_grad, key_error, router_grad, router_error, *small):
    lane_groups, block = sums.shape[1], sums.shape[3]
    key_rows, router_rows = key_grad.shape[1], router_grad.shape[1]
    dk, dr, km, rm = small[3], small[4], small[5], small[7]
    wide = [
        pl.BlockSpec((1, key_rows, TAIL_PARTS * block), lambda i: (0, 0, i)),
        pl.BlockSpec((1, router_rows, TAIL_PARTS * block), lambda i: (0, 0, i)),
    ]

    def whole(shape):
        return pl.BlockSpec(shape, lambda i: (0,) * len(shape))

    outs = [
        (key_grad.shape, f32),
        (router_grad.shape, f32),
        (km.shape, f32),
        (km.shape, f32),
        (dk.shape, bf16),
        (rm.shape, f32),
        (rm.shape, f32),
        ((dk.shape[0], dr.shape[0]), bf16),
    ]
    return pl.pallas_call(
        tail_kernel,
        grid=(lane_groups // TAIL_PARTS,),
        in_specs=[pl.BlockSpec(memory_space=pltpu.VMEM)] * (5 + len(small)),
        out_specs=wide + [whole(shape) for shape, _ in outs[2:]],
        out_shape=[jax.ShapeDtypeStruct(shape, dtype) for shape, dtype in outs],
        name="tail",
    )(*[in_vmem(x) for x in (sums, key_grad, key_error, router_grad, router_error) + small])


def to_all(block, axes, size):
    spread = jnp.broadcast_to(block[None], (size,) + block.shape)
    return lax.all_to_all(spread, axes, 0, 0, tiled=True)


def body(
    key_grad,
    key_error,
    router_grad,
    router_error,
    norm_grad,
    key_basis,
    router_basis,
    key_momentum,
    key_weight,
    router_momentum,
    router_weight,
    norm_momentum,
    norm_weight,
):
    n_z, n_y, n_c, n_x = (lax.axis_size(name) for name in DP + ("shard",))
    plane = n_y * n_c * n_x
    replicas = n_z * n_y * n_c
    rank_size, width = key_basis.shape
    key_rows, router_rows = key_grad.shape[1], router_grad.shape[1]
    norm_vecs, norm_width = norm_grad.shape[1:]
    col_width = key_momentum.shape[1]

    router_end = rank_size + router_rows
    pack = head(key_basis, router_basis, key_grad, key_error, router_grad, router_error, norm_grad)
    pair = lax.all_gather(pack, "c", axis=0, tiled=False)
    half = PACK_ROWS // n_c
    mine = jnp.sum(lax.dynamic_slice_in_dim(pair, lax.axis_index("c") * half, half, 1), axis=0)
    mine = jnp.sum(to_all(mine.astype(bf16), "z", n_z).astype(f32), axis=0)
    spread = to_all(mine, PAIRS, n_y * n_c).reshape(n_y, n_c, half, LANES)
    own = jnp.sum(spread, axis=0).reshape(PACK_ROWS, LANES)

    groups, lane_groups = 2 * rank_size // 8, plane // (2 * rank_size // 8)
    part, sent = mid(
        (groups, lane_groups, 8, width // lane_groups),
        own,
        key_grad,
        key_error,
        router_grad,
        router_error,
        key_momentum.T,
        key_weight.T,
        router_momentum,
        router_weight,
        norm_momentum,
        norm_weight,
    )
    part = part.reshape(plane, 8, width // lane_groups)
    near = lax.ppermute(sent, "shard", [(i, i ^ 1) for i in range(n_x)])
    part = lax.all_to_all(part, PLANE, 0, 0, tiled=True)
    mine = spread_sum(part, n_z)
    mine, near = lax.optimization_barrier((mine, near))
    packs = jnp.stack([sent, near])
    far = lax.ppermute(packs, "shard", [(i, i ^ 2) for i in range(n_x)])
    *lefts, norm_velocity, norm_master, norm_params = side(
        [packs, far], [norm_momentum, norm_weight], replicas, rank_size, router_rows, col_width
    )
    mine = spread_sum(lax.all_to_all(mine, "z", 0, 0, tiled=True), n_y * n_x)
    mine, lefts, norm_velocity, norm_master, norm_params = lax.optimization_barrier(
        (mine, lefts, norm_velocity, norm_master, norm_params)
    )
    sums = lax.all_gather(lax.all_to_all(mine, CHIPS, 0, 0, tiled=True), "c", axis=0, tiled=False)
    sums = sums.reshape(groups, lane_groups, 8, width // lane_groups)
    (key_carry, router_carry, key_velocity, key_master, key_params, router_velocity, router_master, router_params) = (
        tail(
            sums,
            key_grad,
            key_error,
            router_grad,
            router_error,
            *lefts,
            key_momentum.T,
            key_weight.T,
            router_momentum,
            router_weight,
        )
    )

    return (
        key_carry,
        router_carry,
        key_velocity.T,
        key_master.T,
        key_params.T,
        router_velocity,
        router_master,
        router_params.T,
        norm_velocity,
        norm_master,
        norm_params,
    )


def solution(mesh):
    n_dp, n_x = mesh.devices.shape
    fine = Mesh(mesh.devices.reshape(n_dp // 8, 4, 2, n_x), DP + ("shard",))
    return jax.shard_map(
        body,
        mesh=fine,
        in_specs=(
            P(DP, "shard", None),
            P(DP, "shard", None),
            P(DP, "shard", None),
            P(DP, "shard", None),
            P(DP, None, "shard"),
            P(),
            P(),
            P("shard", DP),
            P("shard", DP),
            P("shard", DP),
            P("shard", DP),
            P(None, "shard"),
            P(None, "shard"),
        ),
        out_specs=(
            P(DP, "shard", None),
            P(DP, "shard", None),
            P("shard", DP),
            P("shard", DP),
            P(None, DP),
            P("shard", DP),
            P("shard", DP),
            P(None, DP),
            P(None, "shard"),
            P(None, "shard"),
            P(),
        ),
        check_vma=False,
    )
```

```python
import jax
import jax.numpy as jnp
from jax import lax
from jax.experimental import pallas as pl
from jax.experimental.pallas import tpu as pltpu
from jax.sharding import Mesh, PartitionSpec as P

ROOT_STEPS = 4

highest = lax.Precision.HIGHEST
momentum_decay = 0.9
learning_rate = 0.1
f32 = jnp.float32
bf16 = jnp.bfloat16

DP = ("z", "y", "c")
PAIRS = ("y", "c")
CHIPS = ("y", "shard")
PLANE = ("c",) + CHIPS
LANES = 128
TAIL_PARTS = 2
PACK_ROWS = 48
KEY_AT, ROUTER_AT, NORM_AT = 48, 72, 88


def dot(left, right, left_dim, right_dim):
    return lax.dot_general(left, right, (((left_dim,), (right_dim,)), ((), ())), precision=highest)


def in_halves(left, right, left_dim, right_dim):
    left_high, right_high = left.astype(bf16), right.astype(bf16)
    left_low = (left - left_high.astype(f32)).astype(bf16)
    right_low = (right - right_high.astype(f32)).astype(bf16)
    total = 0.0
    for one, other in ((left_low, right_high), (left_high, right_low), (left_high, right_high)):
        total = total + lax.dot_general(
            one, other, (((left_dim,), (right_dim,)), ((), ())), preferred_element_type=f32
        )
    return total


def in_vmem(array):
    return pltpu.with_memory_space_constraint(array, pltpu.VMEM)


def head_kernel(kb_ref, rb_ref, kg_ref, ke_ref, rg_ref, re_ref, ng_ref, out_ref):
    rank_size, router_rows = kb_ref.shape[0], rg_ref.shape[1]
    norm_vecs, norm_width = ng_ref.shape[1:]
    router_end = rank_size + router_rows

    @pl.when(pl.program_id(0) == 0)
    def _():
        out_ref[...] = jnp.zeros_like(out_ref)
        norm = jnp.concatenate([ng_ref[0].astype(f32), jnp.zeros((8 - norm_vecs, norm_width), f32)], axis=0)
        pieces = router_rows // norm_vecs
        piece = norm_width // pieces
        lane = lax.broadcasted_iota(jnp.int32, (8, LANES), 1)
        for index in range(pieces):
            line = pltpu.roll(norm, (rank_size - index * piece) % norm_width, 1)[:, :LANES]
            line = jnp.where((lane >= rank_size) & (lane < rank_size + piece), line, 0.0)
            for vec in range(norm_vecs):
                row = rank_size + vec * pieces + index
                out_ref[row : row + 1, :] = line[vec : vec + 1]

    merged_key = kg_ref[0].astype(f32) + ke_ref[0]
    merged_router = rg_ref[0].astype(f32) + re_ref[0]
    out_ref[:rank_size, :] += in_halves(kb_ref[...], merged_key, 1, 1)
    out_ref[rank_size:router_end, :rank_size] += in_halves(merged_router, rb_ref[...], 1, 1)


def head(key_basis, router_basis, key_grad, key_error, router_grad, router_error, norm_grad):
    rank_size, width = key_basis.shape
    key_rows, router_rows = key_grad.shape[1], router_grad.shape[1]
    steps = 2
    block = width // steps
    return pl.pallas_call(
        head_kernel,
        grid=(steps,),
        in_specs=[
            pl.BlockSpec((rank_size, block), lambda i: (0, i)),
            pl.BlockSpec((rank_size, block), lambda i: (0, i)),
            pl.BlockSpec((1, key_rows, block), lambda i: (0, 0, i)),
            pl.BlockSpec((1, key_rows, block), lambda i: (0, 0, i)),
            pl.BlockSpec((1, router_rows, block), lambda i: (0, 0, i)),
            pl.BlockSpec((1, router_rows, block), lambda i: (0, 0, i)),
            pl.BlockSpec(norm_grad.shape, lambda i: (0, 0, 0)),
        ],
        out_specs=pl.BlockSpec(memory_space=pltpu.VMEM),
        out_shape=pltpu.VMEM((PACK_ROWS, LANES), f32),
        name="head",
    )(key_basis, router_basis, key_grad, key_error, router_grad, router_error, norm_grad)


def mid_kernel(
    own_ref, kg_ref, ke_ref, rg_ref, re_ref, km_ref, kw_ref, rm_ref, rw_ref, nm_ref, nw_ref, part_ref, sent_ref
):
    groups, lane_groups, lines, block = part_ref.shape
    half, (router_rows, col_width) = groups // 2, rm_ref.shape
    rank_size = half * lines
    key_rows = own_ref[:rank_size, :]
    rout_rows = own_ref[rank_size : rank_size + router_rows, :rank_size]
    for group in range(lane_groups):
        cols = slice(group * block, (group + 1) * block)
        key_part = in_halves(key_rows, kg_ref[0, :, cols].astype(f32) + ke_ref[0, :, cols], 1, 0)
        rout_part = in_halves(rout_rows, rg_ref[0, :, cols].astype(f32) + re_ref[0, :, cols], 0, 0)
        for i in range(half):
            part_ref[i, group] = key_part[i * lines : (i + 1) * lines].astype(bf16)
            part_ref[half + i, group] = rout_part[i * lines : (i + 1) * lines].astype(bf16)
    decay = learning_rate * momentum_decay
    sent_ref[:KEY_AT, :] = own_ref[...]
    sent_ref[KEY_AT:, :] = jnp.zeros((sent_ref.shape[0] - KEY_AT, LANES), f32)
    sent_ref[KEY_AT : KEY_AT + col_width, :] = kw_ref[...] - decay * km_ref[...]
    sent_ref[ROUTER_AT : ROUTER_AT + router_rows, :col_width] = rw_ref[...] - decay * rm_ref[...]
    norm = nw_ref[...] - decay * nm_ref[...]
    norm_vecs, norm_width = norm.shape
    for vec in range(norm_vecs):
        for first in range(0, norm_width, LANES):
            row = NORM_AT + (vec * norm_width + first) // LANES
            sent_ref[row : row + 1, :] = norm[vec : vec + 1, first : first + LANES]


def mid(chunks, *operands):
    return pl.pallas_call(
        mid_kernel,
        in_specs=[pl.BlockSpec(memory_space=pltpu.VMEM)] * len(operands),
        out_specs=[pl.BlockSpec(memory_space=pltpu.VMEM)] * 2,
        out_shape=[pltpu.VMEM(chunks, bf16), pltpu.VMEM((NORM_AT + 16, LANES), f32)],
        name="mid",
    )(*[in_vmem(x) for x in operands])


def square_of_root(gram, replicas):
    scaling = jnp.sqrt(jnp.sum(gram * gram, axis=(0, 1), keepdims=True)) + 1e-06
    rows = lax.broadcasted_iota(jnp.int32, gram.shape, 0)
    identity = (rows == lax.broadcasted_iota(jnp.int32, gram.shape, 1)).astype(f32)
    square_side, root_side = gram / scaling, identity
    for sweep_index in range(ROOT_STEPS):
        if sweep_index == 0:
            middle = 1.5 * identity - 0.5 * square_side
            root_side = middle
        else:
            middle = 1.5 * identity - 0.5 * dot(root_side, square_side, 1, 0)
            root_side = dot(middle, root_side, 1, 0)
        if sweep_index < ROOT_STEPS - 1:
            square_side = dot(square_side, middle, 1, 0)
    return dot(root_side, root_side, 0, 0) / (scaling * replicas)


def norm_rows(lines, start, norm_vecs, norm_width):
    pieces = lines.shape[0] // norm_vecs
    piece = norm_width // pieces
    lane = lax.broadcasted_iota(jnp.int32, lines.shape, 1)
    lines = jnp.where((lane >= start) & (lane < start + piece), lines, 0.0)
    lines = jnp.concatenate([lines, jnp.zeros((lines.shape[0], norm_width - LANES), f32)], axis=1)
    totals = [0.0] * norm_vecs
    for index in range(pieces):
        moved = pltpu.roll(lines, (index * piece - start) % norm_width, 1)
        for vec in range(norm_vecs):
            row = vec * pieces + index
            totals[vec] = totals[vec] + moved[row : row + 1]
    return totals


def side_kernel(replicas, rank_size, router_rows, col_width, *refs):
    packs = [ref.at[i] for ref in refs[:2] for i in range(2)]
    nm_ref, nw_ref, lk_ref, lt_ref, lr_ref, dk_ref, dr_ref, nv_ref, nn_ref, np_ref, wide_ref = refs[2:]
    norm_vecs, norm_width = nm_ref.shape
    router_end = rank_size + router_rows
    shard = lax.axis_index("shard")
    key_rows = [pack[:rank_size, :] for pack in packs]
    rout_rows = [pack[rank_size:router_end, :rank_size] for pack in packs]
    square_key = square_of_root(sum(dot(rows, rows, 1, 1) for rows in key_rows), replicas)
    square_router = square_of_root(sum(dot(rows, rows, 0, 0) for rows in rout_rows), replicas)
    lk_ref[...] = dot(key_rows[0], square_key, 0, 0)
    for distance, pack in enumerate(packs):
        place = lax.bitwise_xor(shard, distance)
        lanes = pl.ds(pl.multiple_of(place * LANES, LANES), LANES)
        lines = pl.ds(pl.multiple_of(place * router_rows, router_rows), router_rows)
        lt_ref[:, lanes] = dot(square_key, key_rows[distance], 0, 0)
        lr_ref[lines, :] = dot(rout_rows[distance], square_router, 1, 0)
        dk_ref[:, lanes] = pack[KEY_AT : KEY_AT + col_width, :]
        dr_ref[lines, :] = pack[ROUTER_AT : ROUTER_AT + router_rows, :]
        means = norm_rows(pack[rank_size:router_end, :], rank_size, norm_vecs, norm_width)
        for vec, mean in enumerate(means):
            mean = mean / replicas
            for first in range(0, norm_width, LANES):
                here = slice(first, first + LANES)
                row = NORM_AT + (vec * norm_width + first) // LANES
                lanes = pl.ds(pl.multiple_of(place * norm_width + first, LANES), LANES)
                wide_ref[vec : vec + 1, lanes] = pack[row : row + 1, :] - learning_rate * mean[:, here]
            if distance == 0:
                velocity = momentum_decay * nm_ref[vec : vec + 1, :] + mean
                nv_ref[vec : vec + 1, :] = velocity
                nn_ref[vec : vec + 1, :] = nw_ref[vec : vec + 1, :] - learning_rate * velocity
    np_ref[...] = wide_ref[...].astype(bf16)


def side(packs, norm_state, replicas, rank_size, router_rows, col_width):
    n_x = 2 * len(packs)
    shapes = [
        (LANES, rank_size),
        (rank_size, n_x * LANES),
        (n_x * router_rows, rank_size),
        (col_width, n_x * LANES),
        (n_x * router_rows, LANES),
    ]
    norm_vecs, norm_width = norm_state[0].shape
    norms = [((norm_vecs, norm_width), f32)] * 2 + [((norm_vecs, n_x * norm_width), bf16)]
    return pl.pallas_call(
        lambda *refs: side_kernel(replicas, rank_size, router_rows, col_width, *refs),
        out_shape=[pltpu.VMEM(shape, f32) for shape in shapes]
        + [jax.ShapeDtypeStruct(shape, dtype) for shape, dtype in norms],
        in_specs=[pl.BlockSpec(memory_space=pltpu.VMEM)] * (len(packs) + 2),
        out_specs=[pl.BlockSpec(memory_space=pltpu.VMEM)] * len(shapes)
        + [pl.BlockSpec(shape, lambda: (0, 0)) for shape, _ in norms],
        scratch_shapes=[pltpu.VMEM(norms[2][0], f32)],
        cost_estimate=pl.CostEstimate(flops=200000000, bytes_accessed=8000000, transcendentals=0),
        name="side",
    )(*[in_vmem(x) for x in packs + norm_state])


def spread_kernel(part_ref, out_ref):
    total = jnp.sum(part_ref[...].astype(f32), axis=0).astype(bf16)
    for place in range(out_ref.shape[0]):
        out_ref[place] = total


def spread_sum(part, size):
    return pl.pallas_call(
        spread_kernel,
        in_specs=[pl.BlockSpec(memory_space=pltpu.VMEM)],
        out_specs=pl.BlockSpec(memory_space=pltpu.VMEM),
        out_shape=pltpu.VMEM((size,) + part.shape[1:], bf16),
        name="spread",
    )(in_vmem(part))


def tail_kernel(
    t_ref, kg_ref, ke_ref, rg_ref, re_ref, lk_ref, lt_ref, lr_ref, dk_ref, dr_ref, km_ref, kw_ref, rm_ref, rw_ref,
    kc_ref, rc_ref, kv_ref, kn_ref, kp_ref, rv_ref, rn_ref, rp_ref,
):
    groups, lane_groups, _, block = t_ref.shape
    rank_size = groups * 4
    half = groups // 2
    router_rows, col_width = rm_ref.shape
    shard = lax.axis_index("shard")
    step = pl.program_id(0)
    own_lines = pl.ds(pl.multiple_of(shard * router_rows, router_rows), router_rows)

    def sums(first, lane_group):
        return jnp.concatenate([t_ref[first + i, lane_group].astype(f32) for i in range(half)], axis=0)

    def apply(left, right):
        high = left.astype(bf16)
        low = (left - high.astype(f32)).astype(bf16)
        terms = [
            lax.dot_general(term, right, (((1,), (0,)), ((), ())), preferred_element_type=f32)
            for term in (high, low)
        ]
        return terms[0] + terms[1]

    for part in range(TAIL_PARTS):
        group = step * TAIL_PARTS + part
        cols = pl.ds(pl.multiple_of(group * block, LANES), block)
        here = slice(part * block, (part + 1) * block)
        left = apply(lk_ref[...], sums(0, group).astype(bf16))
        kc_ref[0, :, here] = kg_ref[0, :, cols].astype(f32) + ke_ref[0, :, cols] - left
        left = apply(lr_ref[own_lines, :], sums(half, group).astype(bf16))
        rc_ref[0, :, here] = rg_ref[0, :, cols].astype(f32) + re_ref[0, :, cols] - left

    @pl.when(step == 0)
    def _():
        place = (lax.axis_index("z") * lax.axis_size("y") + lax.axis_index("y")) * lax.axis_size("c")
        column = (place + lax.axis_index("c")) * col_width
        lane_group = column // block
        offset = column - lane_group * block
        lines = lax.broadcasted_iota(jnp.int32, (block, LANES), 0)
        picks = lines == lax.broadcasted_iota(jnp.int32, (block, LANES), 1) + offset
        picks = picks.astype(f32).astype(bf16)

        def few(first):
            return lax.dot_general(
                sums(first, lane_group).astype(bf16), picks, (((1,), (0,)), ((), ())), preferred_element_type=f32
            )

        few_key, few_router = few(0), few(half)
        approx = dot(few_key, lt_ref[...], 0, 0)[:col_width]
        kp_ref[...] = (dk_ref[...] - learning_rate * approx).astype(bf16)
        own_lanes = pl.ds(pl.multiple_of(shard * LANES, LANES), LANES)
        own = dot(few_key, lt_ref[:, own_lanes], 0, 0)[:col_width]
        velocity = momentum_decay * km_ref[...] + own
        kv_ref[...] = velocity
        kn_ref[...] = kw_ref[...] - learning_rate * velocity
        approx = dr_ref[...] - learning_rate * dot(lr_ref[...], few_router, 1, 0)
        rp_ref[...] = approx.T[:col_width].astype(bf16)
        own = dot(lr_ref[own_lines, :], few_router, 1, 0)[:, :col_width]
        velocity = momentum_decay * rm_ref[...] + own
        rv_ref[...] = velocity
        rn_ref[...] = rw_ref[...] - learning_rate * velocity


def tail(sums, key_grad, key_error, router_grad, router_error, *small):
    lane_groups, block = sums.shape[1], sums.shape[3]
    key_rows, router_rows = key_grad.shape[1], router_grad.shape[1]
    dk, dr, km, rm = small[3], small[4], small[5], small[7]
    wide = [
        pl.BlockSpec((1, key_rows, TAIL_PARTS * block), lambda i: (0, 0, i)),
        pl.BlockSpec((1, router_rows, TAIL_PARTS * block), lambda i: (0, 0, i)),
    ]

    def whole(shape):
        return pl.BlockSpec(shape, lambda i: (0,) * len(shape))

    outs = [
        (key_grad.shape, f32),
        (router_grad.shape, f32),
        (km.shape, f32),
        (km.shape, f32),
        (dk.shape, bf16),
        (rm.shape, f32),
        (rm.shape, f32),
        ((dk.shape[0], dr.shape[0]), bf16),
    ]
    return pl.pallas_call(
        tail_kernel,
        grid=(lane_groups // TAIL_PARTS,),
        in_specs=[pl.BlockSpec(memory_space=pltpu.VMEM)] * (5 + len(small)),
        out_specs=wide + [whole(shape) for shape, _ in outs[2:]],
        out_shape=[jax.ShapeDtypeStruct(shape, dtype) for shape, dtype in outs],
        name="tail",
    )(*[in_vmem(x) for x in (sums, key_grad, key_error, router_grad, router_error) + small])


def to_all(block, axes, size):
    spread = jnp.broadcast_to(block[None], (size,) + block.shape)
    return lax.all_to_all(spread, axes, 0, 0, tiled=True)


def body(
    key_grad,
    key_error,
    router_grad,
    router_error,
    norm_grad,
    key_basis,
    router_basis,
    key_momentum,
    key_weight,
    router_momentum,
    router_weight,
    norm_momentum,
    norm_weight,
):
    n_z, n_y, n_c, n_x = (lax.axis_size(name) for name in DP + ("shard",))
    plane = n_y * n_c * n_x
    replicas = n_z * n_y * n_c
    rank_size, width = key_basis.shape
    key_rows, router_rows = key_grad.shape[1], router_grad.shape[1]
    norm_vecs, norm_width = norm_grad.shape[1:]
    col_width = key_momentum.shape[1]

    router_end = rank_size + router_rows
    pack = head(key_basis, router_basis, key_grad, key_error, router_grad, router_error, norm_grad)
    pair = lax.all_gather(pack, "c", axis=0, tiled=False)
    half = PACK_ROWS // n_c
    mine = jnp.sum(lax.dynamic_slice_in_dim(pair, lax.axis_index("c") * half, half, 1), axis=0)
    mine = jnp.sum(to_all(mine.astype(bf16), "z", n_z).astype(f32), axis=0)
    spread = to_all(mine.astype(bf16), PAIRS, n_y * n_c).astype(f32).reshape(n_y, n_c, half, LANES)
    own = jnp.sum(spread, axis=0).reshape(PACK_ROWS, LANES)

    groups, lane_groups = 2 * rank_size // 8, plane // (2 * rank_size // 8)
    part, sent = mid(
        (groups, lane_groups, 8, width // lane_groups),
        own,
        key_grad,
        key_error,
        router_grad,
        router_error,
        key_momentum.T,
        key_weight.T,
        router_momentum,
        router_weight,
        norm_momentum,
        norm_weight,
    )
    part = part.reshape(plane, 8, width // lane_groups)
    near = lax.ppermute(sent, "shard", [(i, i ^ 1) for i in range(n_x)])
    part = lax.all_to_all(part, PLANE, 0, 0, tiled=True)
    mine = spread_sum(part, n_z)
    mine, near = lax.optimization_barrier((mine, near))
    packs = jnp.stack([sent, near])
    far = lax.ppermute(packs, "shard", [(i, i ^ 2) for i in range(n_x)])
    *lefts, norm_velocity, norm_master, norm_params = side(
        [packs, far], [norm_momentum, norm_weight], replicas, rank_size, router_rows, col_width
    )
    mine = spread_sum(lax.all_to_all(mine, "z", 0, 0, tiled=True), n_y * n_x)
    mine, lefts, norm_velocity, norm_master, norm_params = lax.optimization_barrier(
        (mine, lefts, norm_velocity, norm_master, norm_params)
    )
    sums = lax.all_gather(lax.all_to_all(mine, CHIPS, 0, 0, tiled=True), "c", axis=0, tiled=False)
    sums = sums.reshape(groups, lane_groups, 8, width // lane_groups)
    (key_carry, router_carry, key_velocity, key_master, key_params, router_velocity, router_master, router_params) = (
        tail(
            sums,
            key_grad,
            key_error,
            router_grad,
            router_error,
            *lefts,
            key_momentum.T,
            key_weight.T,
            router_momentum,
            router_weight,
        )
    )

    return (
        key_carry,
        router_carry,
        key_velocity.T,
        key_master.T,
        key_params.T,
        router_velocity,
        router_master,
        router_params.T,
        norm_velocity,
        norm_master,
        norm_params,
    )


def solution(mesh):
    n_dp, n_x = mesh.devices.shape
    fine = Mesh(mesh.devices.reshape(n_dp // 8, 4, 2, n_x), DP + ("shard",))
    return jax.shard_map(
        body,
        mesh=fine,
        in_specs=(
            P(DP, "shard", None),
            P(DP, "shard", None),
            P(DP, "shard", None),
            P(DP, "shard", None),
            P(DP, None, "shard"),
            P(),
            P(),
            P("shard", DP),
            P("shard", DP),
            P("shard", DP),
            P("shard", DP),
            P(None, "shard"),
            P(None, "shard"),
        ),
        out_specs=(
            P(DP, "shard", None),
            P(DP, "shard", None),
            P("shard", DP),
            P("shard", DP),
            P(None, DP),
            P("shard", DP),
            P("shard", DP),
            P(None, DP),
            P(None, "shard"),
            P(None, "shard"),
            P(),
        ),
        check_vma=False,
    )
```
